32 devices in a mesh: row: 4 (over y, core), col: 8 (over z, x).
Axes of the slice: x: 2, y: 2, z: 4, core: 2. Of those that a mesh axis runs over, the one named last changes fastest.
Arguments:
- residual_in: bfloat16 [1024, 2304], P(('row', 'col')), may hold values from -80 to 80
- queries: bfloat16 [1024, 2048], P('row', 'col'), may hold values from -180 to 180
- fresh_cache: bfloat16 [2, 1024, 2048], P(None, 'row', 'col'), may hold values from -6 to 6
- cache_pool: bfloat16 [2, 128, 32, 8192], P(None, 'row', 'col'), may hold values from -6 to 6
- page_table: int32 [4, 32], P('row'), may hold values from 0 to 31, as said below
- context: int32 [4], P('row'), may hold values from 1 to 4096, as said below
- out_weight: bfloat16 [2048, 2304], P('col'), may hold values from -0.375 to 0.375
- norm_gain: bfloat16 [2304], replicated, may hold values from 0.099609375 to 1.8984375
- w_gate: bfloat16 [8, 2304, 5760], P(None, 'row', 'col'), may hold values from -0.125 to 0.125
- w_up: bfloat16 [8, 2304, 5760], P(None, 'row', 'col'), may hold values from -0.125 to 0.125
- w_down: bfloat16 [8, 5760, 2304], P(None, 'col', 'row'), may hold values from -0.078125 to 0.078125
- routes: int32 [1024, 2], P('row'), may hold values from 0 to 7, all different within a row; in each aligned block of 256 rows (0 to 255, 256 to 511, ...) at most 128 rows name the same one
- route_weight: float32 [1024, 2], P('row'), may hold values from 0.25 to 1
- finished_pool: bfloat16 [2, 64, 32, 8192], P(None, 'row', 'col'), may hold values from -6 to 6
- finished_table: int32 [8, 8], P(None, 'row'), may hold values from 0 to 15, as said below
- finished_dest: int32 [8], replicated, may hold values from 0 to 7, each once
Outputs:
- layer_out: bfloat16 [1024, 2304], P(('row', 'col'))
- migrated: bfloat16 [2, 8, 8, 32, 8192], P(None, 'col', None, 'row')
The draws below stay inside these ranges and needn't reach their ends.
Inputs may be any that keep to these rules, and one draw needn't show every extreme that they name: `page_table`: for each index of row, the entries of its 1 request are a permutation of its 32 pages. `context`: every draw has a request with exactly 4096 cached positions. `routes`: each token names 2 different experts. Among the token rows of one index of row no expert is named more than 128 times, and that bound is reached in every draw. `finished_table`: for each index b of row, columns b * 2 to (b + 1) * 2 - 1 over all finished requests are a permutation of 0 to 15. `finished_dest`: A permutation.
All inputs are finite; a program needn't handle non-finite values.
Results may differ from the reference program's by a relative error of at most 0.0095.
Values may be sent and summed in bfloat16 or wider, within the bound.
A program may use at most 256 MiB of HBM per device.

```python
import math
import jax
import jax.numpy as jnp
import numpy as np
from jax import lax

D = 2304
H = 32
HD = 64
E = 8
FF = 5760
TOP = 2
PAGE = 128
MAXP = 32
SPAN = 256
REQ_ROW = 1
FPB = 2
TOK_ROW = 256
TOKENS = 1024
REQS = 4
POOL_ROW = 32
POOL = 128
CAP = 128
FIN = 8
FPAGES = 8
MSLOTS = 16
MPOOL = 64
N_ROW = 4


def attention_pair(key):
    query_key = jax.random.fold_in(key, 11)
    cache_key = jax.random.fold_in(key, 12)
    columns = H * HD
    query_values = jnp.clip(jax.random.normal(query_key, (TOKENS, columns), jnp.float32), -6.0, 6.0) * 2.5
    fresh_values = jnp.clip(jax.random.normal(cache_key, (2, TOKENS, columns), jnp.float32), -6.0, 6.0)
    return (query_values, fresh_values)


def draw_queries(key, part):
    return attention_pair(key)[0].astype(jnp.bfloat16)


def draw_fresh_cache(key, part):
    return attention_pair(key)[1].astype(jnp.bfloat16)


def draw_residual_in(key, part):
    noise_key = jax.random.fold_in(key, 21)
    row_key = jax.random.fold_in(key, 22)
    column_key = jax.random.fold_in(key, 23)
    noise = jnp.clip(jax.random.normal(noise_key, (TOKENS, D), jnp.float32), -5.0, 5.0)
    lowest, highest = (0.32, 3.2)
    row_scale = jnp.exp(jax.random.uniform(row_key, (TOKENS, 1), jnp.float32, math.log(lowest), math.log(highest)))
    column_scale = jnp.exp(jax.random.uniform(column_key, (1, D), jnp.float32, math.log(lowest), math.log(highest)))
    return (noise * row_scale * column_scale).astype(jnp.bfloat16)


def draw_page_table(key, part):
    groups = REQS // REQ_ROW
    subkeys = jax.random.split(jax.random.fold_in(key, 41), groups)
    orders = jax.vmap(lambda subkey: jax.random.permutation(subkey, POOL_ROW))(subkeys)
    return orders.reshape(REQS, MAXP).astype(jnp.int32)


def draw_context(key, part):
    lengths = jax.random.randint(jax.random.fold_in(key, 31), (REQS,), 1, MAXP * PAGE + 1)
    longest = jax.random.randint(jax.random.fold_in(key, 32), (), 0, REQS)
    return jnp.where(jnp.arange(REQS) == longest, MAXP * PAGE, lengths).astype(jnp.int32)


def draw_finished_table(key, part):
    blocks = FPAGES // FPB
    subkeys = jax.random.split(jax.random.fold_in(key, 51), blocks)
    orders = jax.vmap(lambda subkey: jax.random.permutation(subkey, MSLOTS))(subkeys)
    return orders.reshape(blocks, FIN, FPB).transpose(1, 0, 2).reshape(FIN, FPAGES).astype(jnp.int32)


def shard_levels(key, shape, cuts, smallest, top_value):
    loudness = 1.0
    for position, parts in cuts:
        draws = jax.random.uniform(jax.random.fold_in(jax.random.fold_in(key, 6), position), (parts,), jnp.float32, smallest / len(cuts), top_value / len(cuts))
        loudness = loudness * jnp.repeat(jnp.exp(draws), shape[position] // parts).reshape((-1,) + (1,) * (len(shape) - 1 - position))
    return loudness


def shared_out(key, own, number, rows, count, top, most, skew):
    order = jax.random.permutation(key, count)
    heavy_load, ordinary = portions_of(count, rows * top, most, skew, True), portions_of(count, rows * top, most, skew, False)
    places = jnp.arange(count)

    def named(tallies, turn):
        used = int((tallies > 0).sum())
        fixed = max(1, used // 4)
        shifted = fixed + (places - fixed + turn * (used - fixed)) % max(1, count - fixed)
        return jnp.zeros((count,), jnp.int32).at[order[jnp.where(places < fixed, places, shifted)]].set(jnp.asarray(tallies, jnp.int32))

    tallies = jnp.where(number % 4 == 0, named(heavy_load, number // 4), named(ordinary, number - number // 4 - 1))
    mixed = jax.random.permutation(jax.random.fold_in(own, 3), count)
    source_of, taker = mixed[0:count // 2 * 2:2], mixed[1:count // 2 * 2:2]
    room = jnp.minimum(tallies[source_of] - 1, most - tallies[taker]) // 2
    room = jnp.where((source_of == order[0]) | (taker == order[0]) | (tallies[taker] == 0), 0, jnp.maximum(room, 0))
    shifted = jax.random.randint(jax.random.fold_in(own, 4), (count // 2,), 0, 1 << 20) % (room + 1)
    tallies = tallies.at[source_of].add(-shifted).at[taker].add(shifted)
    members = jnp.searchsorted(jnp.cumsum(tallies), jnp.arange(rows * top), side="right").astype(jnp.int32)
    listing = members.reshape(top, rows).T
    listing = listing[jax.random.permutation(jax.random.fold_in(own, 1), rows)]
    turn = jax.random.randint(jax.random.fold_in(own, 2), (rows, 1), 0, top)
    return jnp.take_along_axis(listing, (jnp.arange(top)[None, :] + turn) % top, axis=1)


def portions_of(amount, total, bound, lean, full):
    loads = [(1 << 20) // math.isqrt(standing ** lean) + 1 for standing in range(1, amount + 1)]
    largest = bound if full else min(bound, max(-(-total // amount), total * loads[0] // sum(loads)))
    least = 1 if total - largest >= amount - 1 else 0
    counts, rest = [largest] + [least] * (amount - 1), total - largest - least * (amount - 1)
    while rest > 0:
        candidates = [i for i in range(1, amount) if counts[i] < largest] or [i for i in range(1, amount) if counts[i] < bound]
        mass, remaining = sum([loads[i] for i in candidates]), rest
        for i in candidates:
            more = min(bound - counts[i], max(1, remaining * loads[i] // mass), rest)
            counts[i] = counts[i] + more
            rest = rest - more
    return np.array(counts)


def normal_values(rng, dims, spread, reach, shards=(), held_as=jnp.bfloat16):
    result = jax.random.normal(rng, dims, jnp.float32) * spread
    if len(shards) > 0:
        result = shard_levels(rng, dims, shards, -0.22, 0.18) * result
    return jnp.clip(result, min=-reach, max=reach).astype(held_as)


def setup_inputs(seed: int = 0) -> dict:
    seeds = jax.random.split(jax.random.key(seed), 17)
    residual_in = draw_residual_in(jax.random.fold_in(seeds[16], 71), 0)
    queries = draw_queries(jax.random.fold_in(seeds[16], 71), 0)
    fresh_cache = draw_fresh_cache(jax.random.fold_in(seeds[16], 71), 0)
    cache_pool = normal_values(seeds[3], (2, POOL, H, PAGE * HD), 1.0, 6.0, ((1, 4), (2, 8)))
    page_table = draw_page_table(jax.random.fold_in(seeds[16], 71), 0)
    context = draw_context(jax.random.fold_in(seeds[16], 71), 0)
    out_weight = normal_values(seeds[6], (H * HD, D), (4 * HD) ** -0.5, 0.375, ((0, 8),))
    norm_gain = jnp.clip(1.0 + 0.18 * jax.random.normal(seeds[7], (D,), jnp.float32), 0.099609375, 1.8984375).astype(jnp.bfloat16)
    w_gate = normal_values(seeds[8], (E, D, FF), D ** -0.5, 0.125, ((1, 4), (2, 8)))
    w_up = normal_values(seeds[9], (E, D, FF), D ** -0.5, 0.125, ((1, 4), (2, 8)))
    w_down = normal_values(seeds[10], (E, FF, D), FF ** -0.5, 0.078125, ((1, 8), (2, 4)))
    routes_keys = jax.random.split(jax.random.fold_in(seeds[11], 1), TOKENS // TOK_ROW)
    routes_turns = jax.random.permutation(jax.random.fold_in(seeds[11], 3), TOKENS // TOK_ROW)
    routes = jax.vmap(lambda own, number: shared_out(jax.random.fold_in(seeds[11], 2), own, number, TOK_ROW, E, TOP, CAP, 2))(routes_keys, routes_turns).reshape((TOKENS, TOP))
    route_weight = jnp.clip(0.25 + 0.75 * jax.random.uniform(seeds[12], (TOKENS, TOP), jnp.float32) ** shard_levels(seeds[12], (TOKENS, TOP), ((0, 4),), -0.2, 0.2), 0.25, 1.0)
    finished_pool = normal_values(seeds[13], (2, MPOOL, H, PAGE * HD), 1.0, 6.0, ((1, 4), (2, 8)))
    finished_table = draw_finished_table(jax.random.fold_in(seeds[16], 71), 0)
    finished_dest = jax.random.permutation(seeds[15], FIN).astype(jnp.int32)
    return dict(residual_in=residual_in, queries=queries, fresh_cache=fresh_cache, cache_pool=cache_pool, page_table=page_table, context=context, out_weight=out_weight, norm_gain=norm_gain, w_gate=w_gate, w_up=w_up, w_down=w_down, routes=routes, route_weight=route_weight, finished_pool=finished_pool, finished_table=finished_table, finished_dest=finished_dest)


masked_score = -1e+30
norm_eps = 1e-05

def rms_norm(hidden, norm_gain):
    values = hidden.astype(jnp.float32)
    meansq = lax.optimization_barrier(jnp.mean(values * values, axis=-1, keepdims=True))
    return (values * lax.rsqrt(meansq + norm_eps) * norm_gain.astype(jnp.float32)).astype(jnp.bfloat16)

def request_attention(index, queries, fresh_cache, cache_pool, page_table, context):
    score_scale = 1.0 / math.sqrt(HD)
    group_base = index // REQ_ROW * POOL_ROW
    page_ids = page_table[index] + group_base
    paged = cache_pool[:, page_ids].reshape(2, MAXP, H, PAGE, HD).astype(jnp.float32)
    first_row = index * SPAN
    query_rows = lax.dynamic_slice_in_dim(queries, first_row, SPAN, 0).reshape(SPAN, H, HD).astype(jnp.float32)
    fresh_rows = lax.dynamic_slice_in_dim(fresh_cache, first_row, SPAN, 1).reshape(2, SPAN, H, HD).astype(jnp.float32)
    positions = jnp.arange(MAXP, dtype=jnp.int32)[:, None] * PAGE + jnp.arange(PAGE, dtype=jnp.int32)[None, :]
    causal = jnp.arange(SPAN)[:, None] >= jnp.arange(SPAN)[None, :]
    cached_scores = jnp.einsum('qhd,jhtd->hqjt', query_rows, paged[0]) * score_scale
    cached_scores = jnp.where((positions < context[index])[None, None], cached_scores, masked_score)
    span_scores = jnp.einsum('qhd,khd->hqk', query_rows, fresh_rows[0]) * score_scale
    span_scores = jnp.where(causal[None], span_scores, masked_score)
    highest = jnp.maximum(lax.optimization_barrier(jnp.max(cached_scores, axis=(2, 3))), lax.optimization_barrier(jnp.max(span_scores, axis=2)))
    cached_exp = jnp.exp(cached_scores - highest[:, :, None, None])
    span_exp = jnp.exp(span_scores - highest[:, :, None])
    denominator = lax.optimization_barrier(jnp.sum(cached_exp, axis=(2, 3))) + lax.optimization_barrier(jnp.sum(span_exp, axis=2))
    cached_probs = lax.optimization_barrier((cached_exp / denominator[:, :, None, None]).astype(jnp.bfloat16))
    span_probs = lax.optimization_barrier((span_exp / denominator[:, :, None]).astype(jnp.bfloat16))
    combined = jnp.einsum('hqjt,jhtd->qhd', cached_probs.astype(jnp.float32), paged[1])
    combined = combined + jnp.einsum('hqk,khd->qhd', span_probs.astype(jnp.float32), fresh_rows[1])
    return combined.reshape(SPAN, H * HD).astype(jnp.bfloat16)

def dispatch_targets(route_rows):
    flat_routes = route_rows.reshape(-1)
    onehot_table = (flat_routes[:, None] == jnp.arange(E, dtype=jnp.int32)[None, :]).astype(jnp.int32)
    earlier = jnp.cumsum(onehot_table, axis=0) - onehot_table
    return (flat_routes * CAP + lax.optimization_barrier(jnp.sum(earlier * onehot_table, axis=1))).astype(jnp.int32)

def fill_blocks(normed_rows, targets):
    owners = jnp.zeros((E * CAP,), jnp.int32).at[targets].set(jnp.arange(TOK_ROW * TOP, dtype=jnp.int32) // TOP + 1)
    picked = normed_rows[jnp.maximum(owners - 1, 0)]
    return jnp.where((owners > 0)[:, None], picked, jnp.zeros((), jnp.bfloat16))

def one_expert(operands):
    block_rows, gate_matrix, up_matrix, down_matrix = operands
    gate_sum = jnp.dot(block_rows, gate_matrix, preferred_element_type=jnp.float32)
    up_sum = jnp.dot(block_rows, up_matrix, preferred_element_type=jnp.float32)
    activated = (jax.nn.silu(gate_sum) * up_sum).astype(jnp.bfloat16)
    return jnp.dot(activated, down_matrix, preferred_element_type=jnp.float32)

def reference(residual_in, queries, fresh_cache, cache_pool, page_table, context, out_weight, norm_gain, w_gate, w_up, w_down, routes, route_weight, finished_pool, finished_table, finished_dest):
    request_ids = jnp.arange(REQS, dtype=jnp.int32)
    per_request = lax.map(lambda index: request_attention(index, queries, fresh_cache, cache_pool, page_table, context), request_ids)
    head_out = per_request.reshape(TOKENS, H * HD)
    attended = jnp.dot(head_out, out_weight, preferred_element_type=jnp.float32)
    hidden = lax.optimization_barrier((residual_in.astype(jnp.float32) + attended).astype(jnp.bfloat16))
    normed = rms_norm(hidden, norm_gain)
    grouped_routes = routes.reshape(N_ROW, TOK_ROW, TOP)
    targets = jax.vmap(dispatch_targets)(grouped_routes)
    blocks = jax.vmap(fill_blocks)(normed.reshape(N_ROW, TOK_ROW, D), targets)
    blocks = blocks.reshape(N_ROW, E, CAP, D).transpose(1, 0, 2, 3).reshape(E, N_ROW * CAP, D)
    expert_out = lax.map(one_expert, (blocks, w_gate, w_up, w_down))
    expert_out = expert_out.reshape(E, N_ROW, CAP, D).transpose(1, 0, 2, 3).reshape(N_ROW, E * CAP, D)
    picked = jax.vmap(lambda outputs, indices: outputs[indices])(expert_out, targets).reshape(TOKENS, TOP, D)
    mixture = lax.optimization_barrier(jnp.sum(route_weight.astype(jnp.float32)[:, :, None] * picked, axis=1))
    layer_out = (hidden.astype(jnp.float32) + mixture).astype(jnp.bfloat16)
    block_of_page = jnp.arange(FPAGES, dtype=jnp.int32) // FPB
    pool_pages = (block_of_page[None, :] * MSLOTS + finished_table).astype(jnp.int32)
    gathered = finished_pool[:, pool_pages]
    order_ids = jnp.arange(FIN, dtype=jnp.int32)
    matches = finished_dest[None, :] == order_ids[:, None]
    sources = lax.optimization_barrier(jnp.sum(jnp.where(matches, order_ids[None, :], 0), axis=1)).astype(jnp.int32)
    migrated = gathered[:, sources]
    return (layer_out, migrated)
```

```python
import functools
import math

import jax
import jax.numpy as jnp
from jax import lax
from jax.experimental import pallas as pl
from jax.experimental.pallas import tpu as pltpu
from jax.sharding import PartitionSpec as P

HD = 64
E = 8
TOP = 2
PAGE = 128
MAXP = 32
SPAN = 256
CAP = 128
WIN = CAP + 16

masked_score = -1e30
norm_eps = 1e-05
MESH = pl.DeviceIdType.MESH
f32 = jnp.float32
bf16 = jnp.bfloat16


QB = 128
STEP = 8
PAIRS = PAGE // 2

def attend_body(
    ctx_ref, table_ref, ftable_ref, fdest_ref, q_ref, fresh_ref, weight_ref, cache_ref, pool_ref,
    part_ref, pages_ref,
    raw, picked, flat, heads_buf, out_buf, raw_sems, page_sem,
):
    head_count = cache_ref.shape[2]
    per = 8 // head_count
    finished, blocks = ftable_ref.shape

    def fetch(j, carry):
        page = table_ref[0, j]
        for kv in range(2):
            pltpu.make_async_copy(
                cache_ref.at[kv, page], raw.at[kv, j], raw_sems.at[kv, lax.div(j, STEP)]
            ).start()
        return carry

    lax.fori_loop(0, MAXP, fetch, 0, unroll=STEP)

    def regroup(f, carry):
        dest = fdest_ref[f]
        for kv in range(2):
            for b in range(blocks):
                pltpu.make_async_copy(
                    pool_ref.at[kv, ftable_ref[f, b]], picked.at[dest, kv, b], page_sem
                ).start()
        return carry

    lax.fori_loop(0, finished, regroup, 0)

    def spread(kv, first):
        for i in range(per):
            page = raw[kv, first + i].astype(f32)
            for t in range(PAIRS):
                flat[pl.ds(8 * t + i * head_count, head_count), :] = page[:, t * 128 : (t + 1) * 128]
        for i in range(per):
            for h in range(head_count):
                rows = flat[pl.ds(i * head_count + h, PAIRS, stride=8), :]
                where = pl.ds(pl.multiple_of((first + i) * PAIRS, PAIRS), PAIRS)
                heads_buf[kv, h, where, :] = rows.astype(bf16)

    for chunk in range(MAXP // STEP):
        for kv in range(2):
            pltpu.make_async_copy(
                raw.at[kv, pl.ds(chunk * STEP, STEP)],
                raw.at[kv, pl.ds(chunk * STEP, STEP)],
                raw_sems.at[kv, chunk],
            ).wait()

            @pl.loop(0, STEP // per)
            def _(g):
                spread(kv, chunk * STEP + g * per)

    pltpu.make_async_copy(picked, picked, page_sem).wait()
    to_pages = pltpu.make_async_copy(picked, pages_ref, page_sem)
    to_pages.start()
    context = ctx_ref[0]
    cached = MAXP * PAIRS
    scale = 1.0 / math.sqrt(HD)
    lanes = lax.broadcasted_iota(jnp.int32, (QB, 128), 1)
    low = lanes < HD
    column = lax.broadcasted_iota(jnp.int32, (QB, cached), 1)
    keep = [2 * column + p < context for p in range(2)]
    for block in range(SPAN // QB):
        rows = pl.ds(block * QB, QB)
        causal = (
            block * QB + lax.broadcasted_iota(jnp.int32, (QB, SPAN), 0)
            >= lax.broadcasted_iota(jnp.int32, (QB, SPAN), 1)
        )

        for pair in range((head_count + 1) // 2):
            lane = pl.ds(pair * 128, 128)
            both = q_ref[rows, lane].astype(f32) * scale
            turned = pltpu.roll(both, HD, 1)
            made = []
            for side in range(min(2, head_count - 2 * pair)):
                h = pair * 2 + side
                own = low if side == 0 else jnp.logical_not(low)
                straight = jnp.where(own, both, 0.0).astype(bf16)
                swapped = jnp.where(own, 0.0, turned).astype(bf16)
                by_parity = (straight, swapped) if side == 0 else (swapped, straight)
                keys = heads_buf[0, h]
                values = heads_buf[1, h]
                dims = (((1,), (1,)), ((), ()))
                s = [
                    jnp.where(
                        keep[p],
                        lax.dot_general(by_parity[p], keys, dims, preferred_element_type=f32),
                        masked_score,
                    )
                    for p in range(2)
                ]
                s_new = jnp.where(
                    causal,
                    lax.dot_general(straight, fresh_ref[0, :, lane], dims, preferred_element_type=f32),
                    masked_score,
                )
                highest = jnp.maximum(
                    jnp.max(jnp.maximum(s[0], s[1]), axis=1, keepdims=True),
                    jnp.max(s_new, axis=1, keepdims=True),
                )
                e = [jnp.exp(v - highest) for v in s]
                e_new = jnp.exp(s_new - highest)
                total = jnp.sum(e[0] + e[1], axis=1, keepdims=True) + jnp.sum(
                    e_new, axis=1, keepdims=True
                )
                o = [
                    jnp.dot(e[p].astype(bf16), values, preferred_element_type=f32)
                    for p in range(2)
                ]
                o_new = jnp.dot(
                    e_new.astype(bf16), fresh_ref[1, :, lane], preferred_element_type=f32
                )
                if side == 0:
                    o_cached = o[0] + pltpu.roll(o[1], HD, 1)
                else:
                    o_cached = o[1] + pltpu.roll(o[0], HD, 1)
                made.append((o_cached + o_new) / total)
            out_buf[rows, lane] = jnp.where(low, made[0], made[-1]).astype(bf16)
    part_ref[...] = jnp.dot(out_buf[...], weight_ref[...], preferred_element_type=f32).astype(bf16)
    to_pages.wait()


def attend(queries, fresh_cache, cache_pool, page_table, context, out_weight, finished_pool, finished_table, finished_dest):
    head_count = cache_pool.shape[2]
    extent = cache_pool.shape[3]
    finished, blocks = finished_table.shape
    odd = (head_count % 2) * HD
    queries = jnp.pad(queries, ((0, 0), (0, odd)))
    fresh_cache = jnp.pad(fresh_cache, ((0, 0), (0, 0), (0, odd)))
    out_weight = jnp.pad(out_weight, ((0, odd), (0, 0)))
    width = out_weight.shape[1]
    dma = pltpu.SemaphoreType.DMA
    vmem = pl.BlockSpec(memory_space=pltpu.VMEM)
    smem = pl.BlockSpec(memory_space=pltpu.SMEM)
    hbm = pl.BlockSpec(memory_space=pl.ANY)
    return pl.pallas_call(
        attend_body,
        out_shape=(
            jax.ShapeDtypeStruct((SPAN, width), bf16),
            jax.ShapeDtypeStruct((finished, 2, blocks, head_count, extent), bf16),
        ),
        in_specs=[smem] * 4 + [vmem] * 3 + [hbm] * 2,
        out_specs=(vmem, hbm),
        scratch_shapes=[
            pltpu.VMEM((2, MAXP, head_count, extent), bf16),
            pltpu.VMEM((finished, 2, blocks, head_count, extent), bf16),
            pltpu.VMEM((8 * PAIRS, 128), f32),
            pltpu.VMEM((2, head_count, MAXP * PAIRS, 128), bf16),
            pltpu.VMEM(queries.shape, bf16),
            dma((2, MAXP // STEP)), dma,
        ],
        compiler_params=pltpu.CompilerParams(vmem_limit_bytes=60 << 20),
    )(context, page_table, finished_table, finished_dest, queries, fresh_cache, out_weight, cache_pool, finished_pool)


def regroup(cols, picked):
    moved = lax.all_to_all(picked, "col", split_axis=0, concat_axis=0, tiled=True)
    return moved.reshape((cols, picked.shape[0] // cols) + moved.shape[1:])


def remote(src, dst, sems, index, where):
    copy = pltpu.make_async_remote_copy(
        src_ref=src,
        dst_ref=dst,
        send_sem=sems.at[0, index],
        recv_sem=sems.at[1, index],
        device_id=where,
        device_id_type=MESH,
    )
    copy.start()
    return copy


def greet(rows, cols):
    row, col = lax.axis_index("row"), lax.axis_index("col")
    a, b = col // 2, col % 2
    mate = {"col": a * 2 + (1 - b)}
    line = [{"col": lax.rem(a + 1 + s, cols // 2) * 2 + b} for s in range(cols // 2 - 1)]
    column = [{"row": lax.rem(row + 1 + s, rows)} for s in range(rows - 1)]
    barrier = pltpu.get_barrier_semaphore()
    peers = [mate] + line + column
    for peer in peers:
        pl.semaphore_signal(barrier, inc=1, device_id=peer, device_id_type=MESH)
    pl.semaphore_wait(barrier, len(peers))
    return row, col, mate, line, column


def start_mates(cols, block, mate_buf, mate_sems, mate):
    col = lax.axis_index("col")
    a, b = col // 2, col % 2
    return [
        remote(
            block(lax.rem(a + 1 + s, cols // 2) * 2 + (1 - b)), mate_buf.at[s], mate_sems, s, mate
        )
        for s in range(cols // 2)
    ]


def sum_cols(cols, load, to_mate, mate_buf, pair_buf, far_buf, far_sems, line):
    col = lax.axis_index("col")
    a, b = col // 2, col % 2
    half = cols // 2
    to_far = []
    for s in range(half - 1):
        to_mate[s].wait_recv()
        mine = load(lax.rem(a + 1 + s, half) * 2 + b)
        pair_buf[s] = (mine.astype(f32) + mate_buf[s].astype(f32)).astype(bf16)
        to_far.append(remote(pair_buf.at[s], far_buf.at[s], far_sems, s, line[s]))
    to_mate[half - 1].wait_recv()
    total = load(col).astype(f32) + mate_buf[half - 1].astype(f32)
    for s in range(half - 1):
        to_far[s].wait_recv()
        total = total + far_buf[s].astype(f32)
    return total, to_far


def hidden_body(
    rows, cols, part_ref, res_ref, gain_ref, pages_ref, hidden_ref, tokens_ref, moved_ref,
    mate_buf, pair_buf, far_buf, norm_buf,
    mate_sems, far_sems, row_sems, line_sems, pass_sems, page_sems, own_sem,
):
    half = cols // 2
    group = cols // rows
    depth = tokens_ref.shape[3]
    row, col, mate, line, column = greet(rows, cols)
    a, b = col // 2, col % 2
    copies = start_mates(cols, lambda i: part_ref.at[i], mate_buf, mate_sems, mate)
    to_mate = list(copies)
    pages = [
        remote(
            pages_ref.at[pl.ds(column[s]["row"] * group, group)],
            moved_ref.at[row], page_sems, s, column[s],
        )
        for s in range(rows - 1)
    ]
    own = pltpu.make_async_copy(
        pages_ref.at[pl.ds(row * group, group)], moved_ref.at[row], own_sem
    )
    own.start()
    total, to_far = sum_cols(
        cols, lambda i: part_ref[i], to_mate, mate_buf, pair_buf, far_buf, far_sems, line
    )
    hidden = (res_ref[...].astype(f32) + total).astype(bf16)
    hidden_ref[...] = hidden
    values = hidden.astype(f32)
    meansq = jnp.mean(values * values, axis=-1, keepdims=True)
    normed = (values * lax.rsqrt(meansq + norm_eps) * gain_ref[...].astype(f32)).astype(bf16)
    for r in range(rows):
        norm_buf[r] = normed[:, r * depth : (r + 1) * depth]
    to_row = [
        remote(norm_buf.at[column[s]["row"]], tokens_ref.at[row, col], row_sems, s, column[s])
        for s in range(rows - 1)
    ]
    tokens_ref[row, col] = norm_buf[row]
    for copy in to_row:
        copy.wait_recv()
    block = tokens_ref.at[:, col]
    to_line = [remote(block, block, line_sems, s, line[s]) for s in range(half - 1)]
    passed = [remote(block, block, pass_sems, half - 1, mate)]
    for s in range(half - 1):
        to_line[s].wait_recv()
        origin = lax.rem(a - 1 - s + half, half) * 2 + b
        piece = tokens_ref.at[:, origin]
        passed.append(remote(piece, piece, pass_sems, s, mate))
    for copy in passed:
        copy.wait_recv()
    for copy in pages:
        copy.wait_recv()
    own.wait()
    for copy in to_mate + pages + to_far + to_row + to_line + passed:
        copy.wait_send()


def make_hidden(rows, cols, part, residual, gain, pages, collective_id):
    share, width = residual.shape
    depth = width // rows
    half = cols // 2
    dma = pltpu.SemaphoreType.DMA
    vmem = pl.BlockSpec(memory_space=pltpu.VMEM)
    hbm = pl.BlockSpec(memory_space=pl.ANY)
    return pl.pallas_call(
        functools.partial(hidden_body, rows, cols),
        out_shape=(
            jax.ShapeDtypeStruct((share, width), bf16),
            jax.ShapeDtypeStruct((rows, cols, share, depth), bf16),
            jax.ShapeDtypeStruct((rows, cols // rows) + pages.shape[1:], bf16),
        ),
        in_specs=[vmem, vmem, vmem, hbm],
        out_specs=(vmem, vmem, hbm),
        scratch_shapes=[
            pltpu.VMEM((half, share, width), bf16),
            pltpu.VMEM((half - 1, share, width), bf16),
            pltpu.VMEM((half - 1, share, width), bf16),
            pltpu.VMEM((rows, share, depth), bf16),
            dma((2, half)), dma((2, half)), dma((2, rows)), dma((2, half)), dma((2, half)),
            dma((2, rows)), dma,
        ],
        compiler_params=pltpu.CompilerParams(
            collective_id=collective_id, has_side_effects=True, vmem_limit_bytes=32 << 20
        ),
    )(part, residual, gain, pages)


def mixture_body(
    rows, cols, mixed_ref, out_ref, mate_buf, pair_buf, far_buf, sum_buf,
    mate_sems, far_sems, row_sems,
):
    row, col, mate, line, column = greet(rows, cols)
    to_mate = start_mates(cols, lambda i: mixed_ref.at[:, i], mate_buf, mate_sems, mate)
    total, to_far = sum_cols(
        cols, lambda i: mixed_ref[:, i], to_mate, mate_buf, pair_buf, far_buf, far_sems, line
    )
    sum_buf[...] = total.astype(bf16)
    to_row = [
        remote(sum_buf.at[column[s]["row"]], out_ref.at[row], row_sems, s, column[s])
        for s in range(rows - 1)
    ]
    out_ref[row] = sum_buf[row]
    for copy in to_row:
        copy.wait_recv()
    for copy in to_mate + to_far + to_row:
        copy.wait_send()


def make_mixture(mixed, collective_id):
    rows, cols, share, depth = mixed.shape
    half = cols // 2
    dma = pltpu.SemaphoreType.DMA
    return pl.pallas_call(
        functools.partial(mixture_body, rows, cols),
        out_shape=jax.ShapeDtypeStruct((rows, share, depth), bf16),
        in_specs=[pl.BlockSpec(memory_space=pltpu.VMEM)],
        out_specs=pl.BlockSpec(memory_space=pltpu.VMEM),
        scratch_shapes=[
            pltpu.VMEM((half, rows, share, depth), bf16),
            pltpu.VMEM((half - 1, rows, share, depth), bf16),
            pltpu.VMEM((half - 1, rows, share, depth), bf16),
            pltpu.VMEM((rows, share, depth), bf16),
            dma((2, half)), dma((2, half)), dma((2, rows)),
        ],
        compiler_params=pltpu.CompilerParams(
            collective_id=collective_id, has_side_effects=True, vmem_limit_bytes=32 << 20
        ),
    )(mixed)


def gate_up_body(start_ref, rank_ref, x_ref, gate_ref, up_ref, out_ref, rows_ref):
    e = pl.program_id(0)
    groups, tokens = x_ref.shape[0], x_ref.shape[1]

    @pl.when(e == 0)
    def _():
        out_ref[...] = jnp.zeros_like(out_ref)

    slots = lax.broadcasted_iota(jnp.int32, (WIN, tokens), 0)
    for r in range(groups):
        pick = (slots == rank_ref[0, r : r + 1, :]).astype(f32).astype(bf16)
        rows_ref[r * WIN : (r + 1) * WIN, :] = jnp.dot(
            pick, x_ref[r], preferred_element_type=f32
        ).astype(bf16)
    for side, weight in enumerate((gate_ref, up_ref)):
        sums = jnp.dot(rows_ref[...], weight[0], preferred_element_type=f32).astype(bf16)
        for r in range(groups):
            window = pl.ds(pl.multiple_of(start_ref[r * E + e], 16), WIN)
            out_ref[r, side, window, :] += sums[r * WIN : (r + 1) * WIN]


def gate_up(starts, ranks, x, w_gate, w_up):
    groups, tokens, depth = x.shape
    width = w_gate.shape[2]
    weight_spec = pl.BlockSpec((1, depth, width), lambda e, s: (e, 0, 0))
    return pl.pallas_call(
        gate_up_body,
        grid_spec=pltpu.PrefetchScalarGridSpec(
            num_scalar_prefetch=1,
            grid=(E,),
            in_specs=[
                pl.BlockSpec((1, groups, tokens), lambda e, s: (e, 0, 0)),
                pl.BlockSpec((groups, tokens, depth), lambda e, s: (0, 0, 0)),
                weight_spec,
                weight_spec,
            ],
            out_specs=pl.BlockSpec((groups, 2, tokens * TOP, width), lambda e, s: (0, 0, 0, 0)),
            scratch_shapes=[pltpu.VMEM((groups * WIN, depth), bf16)],
        ),
        out_shape=jax.ShapeDtypeStruct((groups, 2, tokens * TOP, width), bf16),
        compiler_params=pltpu.CompilerParams(vmem_limit_bytes=44 << 20),
    )(starts, ranks, x, w_gate, w_up)


def down_body(start_ref, rank_ref, weight_ref, act_ref, down_ref, out_ref, rows_ref, total_ref):
    e = pl.program_id(0)
    groups, tokens = total_ref.shape[0], total_ref.shape[1]

    @pl.when(e == 0)
    def _():
        total_ref[...] = jnp.zeros_like(total_ref)

    slots = lax.broadcasted_iota(jnp.int32, (WIN, tokens), 0)
    for r in range(groups):
        window = pl.ds(pl.multiple_of(start_ref[r * E + e], 16), WIN)
        rows_ref[r * WIN : (r + 1) * WIN, :] = act_ref[r, window, :]
    outs = lax.dot_general(
        rows_ref[...], down_ref[0], (((1,), (1,)), ((), ())), preferred_element_type=f32
    ).astype(bf16)
    for r in range(groups):
        mix = jnp.where(
            slots == rank_ref[0, r : r + 1, :], weight_ref[0, r : r + 1, :], 0.0
        ).astype(bf16)
        total_ref[r] += lax.dot_general(
            mix,
            outs[r * WIN : (r + 1) * WIN],
            (((0,), (0,)), ((), ())),
            preferred_element_type=f32,
        )

    @pl.when(e == E - 1)
    def _():
        out_ref[...] = total_ref[...].astype(bf16)


def down(starts, ranks, weights, act, w_down):
    groups, pairs, width = act.shape
    tokens = pairs // TOP
    depth = w_down.shape[2]
    w_down = w_down.transpose(0, 2, 1)
    row_spec = pl.BlockSpec((1, groups, tokens), lambda e, s: (e, 0, 0))
    return pl.pallas_call(
        down_body,
        grid_spec=pltpu.PrefetchScalarGridSpec(
            num_scalar_prefetch=1,
            grid=(E,),
            in_specs=[
                row_spec,
                row_spec,
                pl.BlockSpec((groups, pairs, width), lambda e, s: (0, 0, 0)),
                pl.BlockSpec((1, depth, width), lambda e, s: (e, 0, 0)),
            ],
            out_specs=pl.BlockSpec((groups, tokens, depth), lambda e, s: (0, 0, 0)),
            scratch_shapes=[
                pltpu.VMEM((groups * WIN, width), bf16),
                pltpu.VMEM((groups, tokens, depth), f32),
            ],
        ),
        out_shape=jax.ShapeDtypeStruct((groups, tokens, depth), bf16),
        compiler_params=pltpu.CompilerParams(vmem_limit_bytes=44 << 20),
    )(starts, ranks, weights, act, w_down)


CHUNKS = 4


def activate_body(
    part_ref, out_ref, mate_buf, far_out, far_buf,
    mate_send, mate_recv, far_send, far_recv,
    y_send, y_recv, core_send, core_recv, pass_send, pass_recv,
):
    me = lax.axis_index("row")
    y, core = me // 2, me % 2
    mate = y * 2 + (1 - core)
    far = (1 - y) * 2 + core
    rows = part_ref.shape[2] // CHUNKS

    barrier = pltpu.get_barrier_semaphore()
    for peer in (mate, far):
        pl.semaphore_signal(barrier, inc=1, device_id={"row": peer}, device_id_type=MESH)
    pl.semaphore_wait(barrier, 2)

    def chunk(k):
        return pl.ds(k * rows, rows)

    def remote(src, dst, send, recv, peer):
        copy = pltpu.make_async_remote_copy(
            src_ref=src, dst_ref=dst, send_sem=send, recv_sem=recv,
            device_id={"row": peer}, device_id_type=MESH,
        )
        copy.start()
        return copy

    to_mate = [[], []]
    for which, side in ((0, 1 - y), (1, y)):
        for k in range(CHUNKS):
            to_mate[which].append(
                remote(
                    part_ref.at[side * 2 + (1 - core), :, chunk(k)],
                    mate_buf.at[which, :, chunk(k)],
                    mate_send.at[which, k], mate_recv.at[which, k], mate,
                )
            )
    to_far = []
    for k in range(CHUNKS):
        to_mate[0][k].wait_recv()
        far_out[:, chunk(k), :] = (
            part_ref[far, :, chunk(k), :].astype(f32) + mate_buf[0, :, chunk(k), :].astype(f32)
        ).astype(bf16)
        to_far.append(
            remote(
                far_out.at[:, chunk(k)], far_buf.at[:, chunk(k)],
                far_send.at[k], far_recv.at[k], far,
            )
        )
    spread = []
    for k in range(CHUNKS):
        to_mate[1][k].wait_recv()
        to_far[k].wait_recv()
        sums = [
            part_ref[me, s, chunk(k), :].astype(f32)
            + mate_buf[1, s, chunk(k), :].astype(f32)
            + far_buf[s, chunk(k), :].astype(f32)
            for s in range(2)
        ]
        out_ref[me, chunk(k), :] = (sums[0] / (1.0 + jnp.exp(-sums[0])) * sums[1]).astype(bf16)
        block = out_ref.at[me, chunk(k)]
        spread.append(remote(block, block, y_send.at[k], y_recv.at[k], far))
        spread.append(remote(block, block, core_send.at[k], core_recv.at[k], mate))
    passed = []
    for k in range(CHUNKS):
        spread[2 * k].wait_recv()
        block = out_ref.at[far, chunk(k)]
        passed.append(remote(block, block, pass_send.at[k], pass_recv.at[k], mate))
    for k in range(CHUNKS):
        spread[2 * k + 1].wait_recv()
        passed[k].wait_recv()
    for copy in to_mate[0] + to_mate[1] + to_far + spread + passed:
        copy.wait_send()


def activate(part, collective_id):
    groups, _, pairs, width = part.shape
    dma = pltpu.SemaphoreType.DMA
    return pl.pallas_call(
        activate_body,
        out_shape=jax.ShapeDtypeStruct((groups, pairs, width), bf16),
        in_specs=[pl.BlockSpec(memory_space=pltpu.VMEM)],
        out_specs=pl.BlockSpec(memory_space=pltpu.VMEM),
        scratch_shapes=[
            pltpu.VMEM((2, 2, pairs, width), bf16),
            pltpu.VMEM((2, pairs, width), bf16),
            pltpu.VMEM((2, pairs, width), bf16),
            dma((2, CHUNKS)), dma((2, CHUNKS)),
        ] + [dma((CHUNKS,))] * 8,
        compiler_params=pltpu.CompilerParams(
            collective_id=collective_id, has_side_effects=True, vmem_limit_bytes=44 << 20
        ),
    )(part)


def plan(routes, route_weight, groups):
    both = jnp.concatenate([routes.astype(f32), route_weight], axis=1)
    both = lax.all_gather(both, "row", axis=0)
    all_routes = both[:, :, :TOP].astype(jnp.int32)
    all_weights = both[:, :, TOP:]
    experts = jnp.arange(E, dtype=jnp.int32)
    named = all_routes[None, :, :, :] == experts[:, None, None, None]
    member = jnp.any(named, axis=3)
    weights = jnp.sum(jnp.where(named, all_weights[None], 0.0), axis=3)
    tokens = member.shape[2]
    ids = jnp.arange(tokens, dtype=jnp.int32)
    before = (ids[:, None] < ids[None, :]).astype(bf16)
    rank = jnp.einsum(
        "ert,ts->ers", member.astype(bf16), before, preferred_element_type=f32
    ).astype(jnp.int32)
    counts = jnp.sum(member.astype(jnp.int32), axis=2)
    lower = (experts[:, None] > experts[None, :]).astype(jnp.int32)
    offsets = jnp.sum(lower[:, :, None] * counts[None], axis=1)
    starts = jnp.minimum(offsets // 16 * 16, tokens * TOP - WIN)
    ranks = jnp.where(member, rank + (offsets - starts)[:, :, None], -1)
    return starts.T.reshape(-1), ranks, weights


def shards(
    row_count,
    col_count,
    residual_in,
    queries,
    fresh_cache,
    cache_pool,
    page_table,
    context,
    out_weight,
    norm_gain,
    w_gate,
    w_up,
    w_down,
    routes,
    route_weight,
    finished_pool,
    finished_table,
    finished_dest,
):
    share, width = residual_in.shape
    depth = width // row_count
    starts, ranks, weights = plan(routes, route_weight, row_count)
    partial_value, picked = attend(
        queries, fresh_cache, cache_pool, page_table, context, out_weight,
        finished_pool, finished_table, finished_dest,
    )
    pages = regroup(col_count, picked)
    hidden, tokens, moved = make_hidden(
        row_count,
        col_count,
        partial_value.reshape(col_count, share, width),
        residual_in,
        norm_gain.reshape(1, width),
        pages,
        0,
    )
    _, group, requests, sides, blocks, heads, extent = moved.shape
    migrated = moved.transpose(3, 2, 0, 4, 1, 5, 6)
    migrated = migrated.reshape(sides, requests, row_count * blocks, group * heads, extent)
    tokens = tokens.reshape(row_count, col_count * share, depth)
    part = gate_up(starts, ranks, tokens, w_gate, w_up)
    act = activate(part, 1)
    mixed = down(starts, ranks, weights, act, w_down)
    blocks = make_mixture(mixed.reshape(row_count, col_count, share, depth), 2)
    mixture = blocks.transpose(1, 0, 2).reshape(share, width).astype(f32)
    layer_out = (hidden.astype(f32) + mixture).astype(bf16)
    return (layer_out, migrated)


def solution(mesh):
    return jax.shard_map(
        functools.partial(shards, mesh.shape["row"], mesh.shape["col"]),
        mesh=mesh,
        in_specs=(
            P(("row", "col"), None),
            P("row", "col"),
            P(None, "row", "col"),
            P(None, "row", "col", None),
            P("row", None),
            P("row"),
            P("col", None),
            P(),
            P(None, "row", "col"),
            P(None, "row", "col"),
            P(None, "col", "row"),
            P("row", None),
            P("row", None),
            P(None, "row", "col", None),
            P(None, "row"),
            P(),
        ),
        out_specs=(P(("row", "col"), None), P(None, "col", None, "row", None)),
        check_vma=False,
    )
```

```python
import functools
import math

import jax
import jax.numpy as jnp
from jax import lax
from jax.experimental import pallas as pl
from jax.experimental.pallas import tpu as pltpu
from jax.sharding import PartitionSpec as P

HD = 64
E = 8
TOP = 2
PAGE = 128
MAXP = 32
SPAN = 256
CAP = 128
WIN = CAP + 16

masked_score = -1e30
norm_eps = 1e-05
MESH = pl.DeviceIdType.MESH
f32 = jnp.float32
bf16 = jnp.bfloat16


QB = 128
STEP = 8
PAIRS = PAGE // 2

def make_plan(routes, weights):
    tokens = routes.shape[0]
    experts = lax.broadcasted_iota(jnp.int32, (tokens, E), 1)
    named = [routes[:, k : k + 1] == experts for k in range(TOP)]
    member = functools.reduce(jnp.logical_or, named).astype(f32).astype(bf16)
    scaled = sum(jnp.where(named[k], weights[:, k : k + 1], 0.0) for k in range(TOP)).astype(bf16)
    first = lax.broadcasted_iota(jnp.int32, (tokens, tokens), 0)
    second = lax.broadcasted_iota(jnp.int32, (tokens, tokens), 1)
    before = (first < second).astype(f32).astype(bf16)
    same = (first == second).astype(f32).astype(bf16)
    dims = (((0,), (0,)), ((), ()))
    rank = lax.dot_general(member, before, dims, preferred_element_type=f32)
    is_member = lax.dot_general(member, same, dims, preferred_element_type=f32)
    by_expert = lax.dot_general(scaled, same, dims, preferred_element_type=f32)
    lower = (
        lax.broadcasted_iota(jnp.int32, (E, E), 0) > lax.broadcasted_iota(jnp.int32, (E, E), 1)
    ).astype(f32).astype(bf16)
    ahead = jnp.dot(lower, is_member.astype(bf16), preferred_element_type=f32)
    offsets = jnp.sum(ahead, axis=1, keepdims=True)
    starts = jnp.minimum(jnp.floor(offsets * (1.0 / 16)) * 16.0, tokens * TOP - WIN)
    ranks = jnp.where(is_member > 0.5, rank + (offsets - starts), -1.0)
    return jnp.concatenate([ranks, by_expert, jnp.broadcast_to(starts, ranks.shape)], axis=0)


def attend_body(
    ctx_ref, table_ref, ftable_ref, fdest_ref, q_ref, fresh_ref, weight_ref, routes_ref,
    route_weight_ref, cache_ref, pool_ref, part_ref, pages_ref, plan_ref,
    raw, picked, flat, heads_buf, out_buf, raw_sems, page_sem,
):
    head_count = cache_ref.shape[2]
    per = 8 // head_count
    finished, blocks = ftable_ref.shape

    def fetch(j, carry):
        page = table_ref[0, j]
        for kv in range(2):
            pltpu.make_async_copy(
                cache_ref.at[kv, page], raw.at[kv, j], raw_sems.at[kv, lax.div(j, STEP)]
            ).start()
        return carry

    lax.fori_loop(0, MAXP, fetch, 0, unroll=STEP)

    def regroup(f, carry):
        dest = fdest_ref[f]
        for kv in range(2):
            for b in range(blocks):
                pltpu.make_async_copy(
                    pool_ref.at[kv, ftable_ref[f, b]], picked.at[dest, kv, b], page_sem
                ).start()
        return carry

    lax.fori_loop(0, finished, regroup, 0)

    plan_ref[...] = make_plan(routes_ref[...], route_weight_ref[...])

    def spread(kv, first):
        for i in range(per):
            page = raw[kv, first + i].astype(f32)
            for t in range(PAIRS):
                flat[pl.ds(8 * t + i * head_count, head_count), :] = page[:, t * 128 : (t + 1) * 128]
        for i in range(per):
            for h in range(head_count):
                rows = flat[pl.ds(i * head_count + h, PAIRS, stride=8), :]
                where = pl.ds(pl.multiple_of((first + i) * PAIRS, PAIRS), PAIRS)
                heads_buf[kv, h, where, :] = rows.astype(bf16)

    for chunk in range(MAXP // STEP):
        for kv in range(2):
            pltpu.make_async_copy(
                raw.at[kv, pl.ds(chunk * STEP, STEP)],
                raw.at[kv, pl.ds(chunk * STEP, STEP)],
                raw_sems.at[kv, chunk],
            ).wait()

            @pl.loop(0, STEP // per)
            def _(g):
                spread(kv, chunk * STEP + g * per)

    pltpu.make_async_copy(picked, picked, page_sem).wait()
    to_pages = pltpu.make_async_copy(picked, pages_ref, page_sem)
    to_pages.start()
    context = ctx_ref[0]
    cached = MAXP * PAIRS
    scale = 1.0 / math.sqrt(HD)
    lanes = lax.broadcasted_iota(jnp.int32, (QB, 128), 1)
    low = lanes < HD
    column = lax.broadcasted_iota(jnp.int32, (QB, cached), 1)
    keep = [2 * column + p < context for p in range(2)]
    for block in range(SPAN // QB):
        rows = pl.ds(block * QB, QB)
        causal = (
            block * QB + lax.broadcasted_iota(jnp.int32, (QB, SPAN), 0)
            >= lax.broadcasted_iota(jnp.int32, (QB, SPAN), 1)
        )

        for pair in range((head_count + 1) // 2):
            lane = pl.ds(pair * 128, 128)
            both = q_ref[rows, lane].astype(f32) * scale
            turned = pltpu.roll(both, HD, 1)
            made = []
            for side in range(min(2, head_count - 2 * pair)):
                h = pair * 2 + side
                own = low if side == 0 else jnp.logical_not(low)
                straight = jnp.where(own, both, 0.0).astype(bf16)
                swapped = jnp.where(own, 0.0, turned).astype(bf16)
                by_parity = (straight, swapped) if side == 0 else (swapped, straight)
                keys = heads_buf[0, h]
                values = heads_buf[1, h]
                dims = (((1,), (1,)), ((), ()))
                s = [
                    jnp.where(
                        keep[p],
                        lax.dot_general(by_parity[p], keys, dims, preferred_element_type=f32),
                        masked_score,
                    )
                    for p in range(2)
                ]
                s_new = jnp.where(
                    causal,
                    lax.dot_general(straight, fresh_ref[0, :, lane], dims, preferred_element_type=f32),
                    masked_score,
                )
                highest = jnp.maximum(
                    jnp.max(jnp.maximum(s[0], s[1]), axis=1, keepdims=True),
                    jnp.max(s_new, axis=1, keepdims=True),
                )
                e = [jnp.exp(v - highest) for v in s]
                e_new = jnp.exp(s_new - highest)
                total = jnp.sum(e[0] + e[1], axis=1, keepdims=True) + jnp.sum(
                    e_new, axis=1, keepdims=True
                )
                o = [
                    jnp.dot(e[p].astype(bf16), values, preferred_element_type=f32)
                    for p in range(2)
                ]
                o_new = jnp.dot(
                    e_new.astype(bf16), fresh_ref[1, :, lane], preferred_element_type=f32
                )
                if side == 0:
                    o_cached = o[0] + pltpu.roll(o[1], HD, 1)
                else:
                    o_cached = o[1] + pltpu.roll(o[0], HD, 1)
                made.append((o_cached + o_new) / total)
            out_buf[rows, lane] = jnp.where(low, made[0], made[-1]).astype(bf16)
    part_ref[...] = jnp.dot(out_buf[...], weight_ref[...], preferred_element_type=f32).astype(bf16)
    to_pages.wait()


def attend(
    queries, fresh_cache, cache_pool, page_table, context, out_weight, routes, route_weight,
    finished_pool, finished_table, finished_dest,
):
    head_count = cache_pool.shape[2]
    extent = cache_pool.shape[3]
    finished, blocks = finished_table.shape
    odd = (head_count % 2) * HD
    queries = jnp.pad(queries, ((0, 0), (0, odd)))
    fresh_cache = jnp.pad(fresh_cache, ((0, 0), (0, 0), (0, odd)))
    out_weight = jnp.pad(out_weight, ((0, odd), (0, 0)))
    width = out_weight.shape[1]
    dma = pltpu.SemaphoreType.DMA
    vmem = pl.BlockSpec(memory_space=pltpu.VMEM)
    smem = pl.BlockSpec(memory_space=pltpu.SMEM)
    hbm = pl.BlockSpec(memory_space=pl.ANY)
    return pl.pallas_call(
        attend_body,
        out_shape=(
            jax.ShapeDtypeStruct((SPAN, width), bf16),
            jax.ShapeDtypeStruct((finished, 2, blocks, head_count, extent), bf16),
            jax.ShapeDtypeStruct((3 * E, SPAN), f32),
        ),
        in_specs=[smem] * 4 + [vmem] * 5 + [hbm] * 2,
        out_specs=(vmem, hbm, vmem),
        scratch_shapes=[
            pltpu.VMEM((2, MAXP, head_count, extent), bf16),
            pltpu.VMEM((finished, 2, blocks, head_count, extent), bf16),
            pltpu.VMEM((8 * PAIRS, 128), f32),
            pltpu.VMEM((2, head_count, MAXP * PAIRS, 128), bf16),
            pltpu.VMEM(queries.shape, bf16),
            dma((2, MAXP // STEP)), dma,
        ],
        compiler_params=pltpu.CompilerParams(vmem_limit_bytes=60 << 20),
    )(context, page_table, finished_table, finished_dest, queries, fresh_cache, out_weight,
      routes, route_weight, cache_pool, finished_pool)


def remote(src, dst, sems, index, where):
    copy = pltpu.make_async_remote_copy(
        src_ref=src,
        dst_ref=dst,
        send_sem=sems.at[0, index],
        recv_sem=sems.at[1, index],
        device_id=where,
        device_id_type=MESH,
    )
    copy.start()
    return copy


def greet(rows, cols):
    row, col = lax.axis_index("row"), lax.axis_index("col")
    a, b = col // 2, col % 2
    mate = {"col": a * 2 + (1 - b)}
    line = [{"col": lax.rem(a + 1 + s, cols // 2) * 2 + b} for s in range(cols // 2 - 1)]
    column = [{"row": lax.rem(row + 1 + s, rows)} for s in range(rows - 1)]
    barrier = pltpu.get_barrier_semaphore()
    peers = [mate] + line + column
    for peer in peers:
        pl.semaphore_signal(barrier, inc=1, device_id=peer, device_id_type=MESH)
    pl.semaphore_wait(barrier, len(peers))
    return row, col, mate, line, column


def start_mates(cols, block, mate_buf, mate_sems, mate):
    col = lax.axis_index("col")
    a, b = col // 2, col % 2
    return [
        remote(
            block(lax.rem(a + 1 + s, cols // 2) * 2 + (1 - b)), mate_buf.at[s], mate_sems, s, mate
        )
        for s in range(cols // 2)
    ]


def sum_cols(cols, load, to_mate, mate_buf, pair_buf, far_buf, far_sems, line):
    col = lax.axis_index("col")
    a, b = col // 2, col % 2
    half = cols // 2
    to_far = []
    for s in range(half - 1):
        to_mate[s].wait_recv()
        mine = load(lax.rem(a + 1 + s, half) * 2 + b)
        pair_buf[s] = (mine.astype(f32) + mate_buf[s].astype(f32)).astype(bf16)
        to_far.append(remote(pair_buf.at[s], far_buf.at[s], far_sems, s, line[s]))
    to_mate[half - 1].wait_recv()
    total = load(col).astype(f32) + mate_buf[half - 1].astype(f32)
    for s in range(half - 1):
        to_far[s].wait_recv()
        total = total + far_buf[s].astype(f32)
    return total, to_far


def hidden_body(
    rows, cols, part_ref, res_ref, gain_ref, plan_ref, hidden_ref, tokens_ref, plans_ref,
    mate_buf, pair_buf, far_buf, norm_buf,
    mate_sems, far_sems, row_sems, line_sems, pass_sems, plan_sems,
):
    half = cols // 2
    depth = tokens_ref.shape[3]
    row, col, mate, line, column = greet(rows, cols)
    a, b = col // 2, col % 2
    copies = start_mates(cols, lambda i: part_ref.at[i], mate_buf, mate_sems, mate)
    to_mate = list(copies)
    plans = [
        remote(plan_ref, plans_ref.at[row], plan_sems, s, column[s]) for s in range(rows - 1)
    ]
    plans_ref[row] = plan_ref[...]
    total, to_far = sum_cols(
        cols, lambda i: part_ref[i], to_mate, mate_buf, pair_buf, far_buf, far_sems, line
    )
    hidden = (res_ref[...].astype(f32) + total).astype(bf16)
    hidden_ref[...] = hidden
    values = hidden.astype(f32)
    meansq = jnp.mean(values * values, axis=-1, keepdims=True)
    normed = (values * lax.rsqrt(meansq + norm_eps) * gain_ref[...].astype(f32)).astype(bf16)
    for r in range(rows):
        norm_buf[r] = normed[:, r * depth : (r + 1) * depth]
    to_row = [
        remote(norm_buf.at[column[s]["row"]], tokens_ref.at[row, col], row_sems, s, column[s])
        for s in range(rows - 1)
    ]
    tokens_ref[row, col] = norm_buf[row]
    for copy in to_row:
        copy.wait_recv()
    block = tokens_ref.at[:, col]
    to_line = [remote(block, block, line_sems, s, line[s]) for s in range(half - 1)]
    passed = [remote(block, block, pass_sems, half - 1, mate)]
    for s in range(half - 1):
        to_line[s].wait_recv()
        origin = lax.rem(a - 1 - s + half, half) * 2 + b
        piece = tokens_ref.at[:, origin]
        passed.append(remote(piece, piece, pass_sems, s, mate))
    for copy in passed:
        copy.wait_recv()
    for copy in plans:
        copy.wait_recv()
    for copy in to_mate + plans + to_far + to_row + to_line + passed:
        copy.wait_send()


def make_hidden(rows, cols, part, residual, gain, plan, collective_id):
    share, width = residual.shape
    depth = width // rows
    half = cols // 2
    dma = pltpu.SemaphoreType.DMA
    vmem = pl.BlockSpec(memory_space=pltpu.VMEM)
    return pl.pallas_call(
        functools.partial(hidden_body, rows, cols),
        out_shape=(
            jax.ShapeDtypeStruct((share, width), bf16),
            jax.ShapeDtypeStruct((rows, cols, share, depth), bf16),
            jax.ShapeDtypeStruct((rows,) + plan.shape, f32),
        ),
        in_specs=[vmem] * 4,
        out_specs=(vmem, vmem, vmem),
        scratch_shapes=[
            pltpu.VMEM((half, share, width), bf16),
            pltpu.VMEM((half - 1, share, width), bf16),
            pltpu.VMEM((half - 1, share, width), bf16),
            pltpu.VMEM((rows, share, depth), bf16),
            dma((2, half)), dma((2, half)), dma((2, rows)), dma((2, half)), dma((2, half)),
            dma((2, rows)),
        ],
        compiler_params=pltpu.CompilerParams(
            collective_id=collective_id, has_side_effects=True, vmem_limit_bytes=32 << 20
        ),
    )(part, residual, gain, plan)


def mixture_body(
    rows, cols, mixed_ref, pages_ref, out_ref, moved_ref, mate_buf, pair_buf, far_buf, sum_buf,
    mate_sems, far_sems, row_sems, page_sems,
):
    row, col, mate, line, column = greet(rows, cols)
    group = cols // rows
    pages = [
        remote(
            pages_ref.at[pl.ds(column[s]["row"] * group, group)],
            moved_ref.at[row], page_sems, s, column[s],
        )
        for s in range(rows - 1)
    ]
    for i in range(group):
        moved_ref[row, i] = pages_ref[row * group + i]
    to_mate = start_mates(cols, lambda i: mixed_ref.at[:, i], mate_buf, mate_sems, mate)
    total, to_far = sum_cols(
        cols, lambda i: mixed_ref[:, i], to_mate, mate_buf, pair_buf, far_buf, far_sems, line
    )
    sum_buf[...] = total.astype(bf16)
    to_row = [
        remote(sum_buf.at[column[s]["row"]], out_ref.at[row], row_sems, s, column[s])
        for s in range(rows - 1)
    ]
    out_ref[row] = sum_buf[row]
    for copy in to_row:
        copy.wait_recv()
    for copy in pages:
        copy.wait_recv()
    for copy in to_mate + to_far + to_row + pages:
        copy.wait_send()


def make_mixture(mixed, pages, collective_id):
    rows, cols, share, depth = mixed.shape
    half = cols // 2
    dma = pltpu.SemaphoreType.DMA
    return pl.pallas_call(
        functools.partial(mixture_body, rows, cols),
        out_shape=(
            jax.ShapeDtypeStruct((rows, share, depth), bf16),
            jax.ShapeDtypeStruct((rows, cols // rows) + pages.shape[1:], bf16),
        ),
        in_specs=[pl.BlockSpec(memory_space=pltpu.VMEM)] * 2,
        out_specs=(pl.BlockSpec(memory_space=pltpu.VMEM),) * 2,
        scratch_shapes=[
            pltpu.VMEM((half, rows, share, depth), bf16),
            pltpu.VMEM((half - 1, rows, share, depth), bf16),
            pltpu.VMEM((half - 1, rows, share, depth), bf16),
            pltpu.VMEM((rows, share, depth), bf16),
            dma((2, half)), dma((2, half)), dma((2, rows)), dma((2, rows)),
        ],
        compiler_params=pltpu.CompilerParams(
            collective_id=collective_id, has_side_effects=True, vmem_limit_bytes=32 << 20
        ),
    )(mixed, pages)


def gate_up_body(start_ref, plan_ref, x_ref, gate_ref, up_ref, out_ref, rows_ref):
    e = pl.program_id(0)
    groups, tokens = x_ref.shape[0], x_ref.shape[1]

    @pl.when(e == 0)
    def _():
        out_ref[...] = jnp.zeros_like(out_ref)

    slots = lax.broadcasted_iota(jnp.int32, (WIN, tokens), 0).astype(f32)
    for r in range(groups):
        pick = (slots == plan_ref[r, pl.ds(e, 1), :]).astype(f32).astype(bf16)
        rows_ref[r * WIN : (r + 1) * WIN, :] = jnp.dot(
            pick, x_ref[r], preferred_element_type=f32
        ).astype(bf16)
    for side, weight in enumerate((gate_ref, up_ref)):
        sums = jnp.dot(rows_ref[...], weight[0], preferred_element_type=f32).astype(bf16)
        for r in range(groups):
            window = pl.ds(pl.multiple_of(start_ref[r * E + e], 16), WIN)
            out_ref[r, side, window, :] += sums[r * WIN : (r + 1) * WIN]


def gate_up(starts, plans, x, w_gate, w_up):
    groups, tokens, depth = x.shape
    width = w_gate.shape[2]
    weight_spec = pl.BlockSpec((1, depth, width), lambda e, s: (e, 0, 0))
    return pl.pallas_call(
        gate_up_body,
        grid_spec=pltpu.PrefetchScalarGridSpec(
            num_scalar_prefetch=1,
            grid=(E,),
            in_specs=[
                pl.BlockSpec(plans.shape, lambda e, s: (0, 0, 0)),
                pl.BlockSpec((groups, tokens, depth), lambda e, s: (0, 0, 0)),
                weight_spec,
                weight_spec,
            ],
            out_specs=pl.BlockSpec((groups, 2, tokens * TOP, width), lambda e, s: (0, 0, 0, 0)),
            scratch_shapes=[pltpu.VMEM((groups * WIN, depth), bf16)],
        ),
        out_shape=jax.ShapeDtypeStruct((groups, 2, tokens * TOP, width), bf16),
        compiler_params=pltpu.CompilerParams(vmem_limit_bytes=44 << 20),
    )(starts, plans, x, w_gate, w_up)


def down_body(start_ref, plan_ref, act_ref, down_ref, out_ref, rows_ref, total_ref):
    e = pl.program_id(0)
    groups, tokens = total_ref.shape[0], total_ref.shape[1]

    @pl.when(e == 0)
    def _():
        total_ref[...] = jnp.zeros_like(total_ref)

    slots = lax.broadcasted_iota(jnp.int32, (WIN, tokens), 0).astype(f32)
    for r in range(groups):
        window = pl.ds(pl.multiple_of(start_ref[r * E + e], 16), WIN)
        rows_ref[r * WIN : (r + 1) * WIN, :] = act_ref[r, window, :]
    outs = lax.dot_general(
        rows_ref[...], down_ref[0], (((1,), (1,)), ((), ())), preferred_element_type=f32
    ).astype(bf16)
    for r in range(groups):
        mix = jnp.where(
            slots == plan_ref[r, pl.ds(e, 1), :], plan_ref[r, pl.ds(E + e, 1), :], 0.0
        ).astype(bf16)
        total_ref[r] += lax.dot_general(
            mix,
            outs[r * WIN : (r + 1) * WIN],
            (((0,), (0,)), ((), ())),
            preferred_element_type=f32,
        )

    @pl.when(e == E - 1)
    def _():
        out_ref[...] = total_ref[...].astype(bf16)


def down(starts, plans, act, w_down):
    groups, pairs, width = act.shape
    tokens = pairs // TOP
    depth = w_down.shape[2]
    w_down = w_down.transpose(0, 2, 1)
    return pl.pallas_call(
        down_body,
        grid_spec=pltpu.PrefetchScalarGridSpec(
            num_scalar_prefetch=1,
            grid=(E,),
            in_specs=[
                pl.BlockSpec(plans.shape, lambda e, s: (0, 0, 0)),
                pl.BlockSpec((groups, pairs, width), lambda e, s: (0, 0, 0)),
                pl.BlockSpec((1, depth, width), lambda e, s: (e, 0, 0)),
            ],
            out_specs=pl.BlockSpec((groups, tokens, depth), lambda e, s: (0, 0, 0)),
            scratch_shapes=[
                pltpu.VMEM((groups * WIN, width), bf16),
                pltpu.VMEM((groups, tokens, depth), f32),
            ],
        ),
        out_shape=jax.ShapeDtypeStruct((groups, tokens, depth), bf16),
        compiler_params=pltpu.CompilerParams(vmem_limit_bytes=44 << 20),
    )(starts, plans, act, w_down)


CHUNKS = 4


def activate_body(
    cols, part_ref, pages_ref, out_ref, arrived_ref, mate_buf, far_out, far_buf, page_sems,
    mate_send, mate_recv, far_send, far_recv,
    y_send, y_recv, core_send, core_recv, pass_send, pass_recv,
):
    me = lax.axis_index("row")
    y, core = me // 2, me % 2
    mate = y * 2 + (1 - core)
    far = (1 - y) * 2 + core
    rows = part_ref.shape[2] // CHUNKS

    barrier = pltpu.get_barrier_semaphore()
    col = lax.axis_index("col")
    others = [lax.rem(col + 1 + s, cols) for s in range(cols - 1)]
    peers = [{"row": mate}, {"row": far}] + [{"col": c} for c in others]
    for peer in peers:
        pl.semaphore_signal(barrier, inc=1, device_id=peer, device_id_type=MESH)
    pl.semaphore_wait(barrier, len(peers))

    def chunk(k):
        return pl.ds(k * rows, rows)

    def to_row(src, dst, send, recv, peer):
        copy = pltpu.make_async_remote_copy(
            src_ref=src, dst_ref=dst, send_sem=send, recv_sem=recv,
            device_id={"row": peer}, device_id_type=MESH,
        )
        copy.start()
        return copy

    to_mate = [[], []]
    for which, side in ((0, 1 - y), (1, y)):
        for k in range(CHUNKS):
            to_mate[which].append(
                to_row(
                    part_ref.at[side * 2 + (1 - core), :, chunk(k)],
                    mate_buf.at[which, :, chunk(k)],
                    mate_send.at[which, k], mate_recv.at[which, k], mate,
                )
            )
    pages = [
        remote(pages_ref.at[c], arrived_ref.at[col], page_sems, s, {"col": c})
        for s, c in enumerate(others)
    ]
    arrived_ref[col] = pages_ref[col]
    to_far = []
    for k in range(CHUNKS):
        to_mate[0][k].wait_recv()
        far_out[:, chunk(k), :] = (
            part_ref[far, :, chunk(k), :].astype(f32) + mate_buf[0, :, chunk(k), :].astype(f32)
        ).astype(bf16)
        to_far.append(
            to_row(
                far_out.at[:, chunk(k)], far_buf.at[:, chunk(k)],
                far_send.at[k], far_recv.at[k], far,
            )
        )
    spread = []
    for k in range(CHUNKS):
        to_mate[1][k].wait_recv()
        to_far[k].wait_recv()
        sums = [
            part_ref[me, s, chunk(k), :].astype(f32)
            + mate_buf[1, s, chunk(k), :].astype(f32)
            + far_buf[s, chunk(k), :].astype(f32)
            for s in range(2)
        ]
        out_ref[me, chunk(k), :] = (sums[0] / (1.0 + jnp.exp(-sums[0])) * sums[1]).astype(bf16)
        block = out_ref.at[me, chunk(k)]
        spread.append(to_row(block, block, y_send.at[k], y_recv.at[k], far))
        spread.append(to_row(block, block, core_send.at[k], core_recv.at[k], mate))
    passed = []
    for k in range(CHUNKS):
        spread[2 * k].wait_recv()
        block = out_ref.at[far, chunk(k)]
        passed.append(to_row(block, block, pass_send.at[k], pass_recv.at[k], mate))
    for k in range(CHUNKS):
        spread[2 * k + 1].wait_recv()
        passed[k].wait_recv()
    for copy in pages:
        copy.wait_recv()
    for copy in to_mate[0] + to_mate[1] + to_far + spread + passed + pages:
        copy.wait_send()


def activate(cols, part, pages, collective_id):
    groups, _, pairs, width = part.shape
    dma = pltpu.SemaphoreType.DMA
    return pl.pallas_call(
        functools.partial(activate_body, cols),
        out_shape=(
            jax.ShapeDtypeStruct((groups, pairs, width), bf16),
            jax.ShapeDtypeStruct(pages.shape, bf16),
        ),
        in_specs=[pl.BlockSpec(memory_space=pltpu.VMEM)] * 2,
        out_specs=(pl.BlockSpec(memory_space=pltpu.VMEM),) * 2,
        scratch_shapes=[
            pltpu.VMEM((2, 2, pairs, width), bf16),
            pltpu.VMEM((2, pairs, width), bf16),
            pltpu.VMEM((2, pairs, width), bf16),
            dma((2, cols)), dma((2, CHUNKS)), dma((2, CHUNKS)),
        ] + [dma((CHUNKS,))] * 8,
        compiler_params=pltpu.CompilerParams(
            collective_id=collective_id, has_side_effects=True, vmem_limit_bytes=44 << 20
        ),
    )(part, pages)


def shards(
    row_count,
    col_count,
    residual_in,
    queries,
    fresh_cache,
    cache_pool,
    page_table,
    context,
    out_weight,
    norm_gain,
    w_gate,
    w_up,
    w_down,
    routes,
    route_weight,
    finished_pool,
    finished_table,
    finished_dest,
):
    share, width = residual_in.shape
    depth = width // row_count
    partial_value, picked, plan = attend(
        queries, fresh_cache, cache_pool, page_table, context, out_weight, routes, route_weight,
        finished_pool, finished_table, finished_dest,
    )
    hidden, tokens, plans = make_hidden(
        row_count,
        col_count,
        partial_value.reshape(col_count, share, width),
        residual_in,
        norm_gain.reshape(1, width),
        plan,
        0,
    )
    starts = plans[:, 2 * E :, 0].astype(jnp.int32).reshape(-1)
    tokens = tokens.reshape(row_count, col_count * share, depth)
    part = gate_up(starts, plans, tokens, w_gate, w_up)
    pages = picked.reshape((col_count, picked.shape[0] // col_count) + picked.shape[1:])
    act, arrived = activate(col_count, part, pages, 1)
    mixed = down(starts, plans, act, w_down)
    blocks, moved = make_mixture(
        mixed.reshape(row_count, col_count, share, depth), arrived, 2
    )
    _, group, requests, sides, block_count, heads, extent = moved.shape
    migrated = moved.transpose(3, 2, 0, 4, 1, 5, 6)
    migrated = migrated.reshape(sides, requests, row_count * block_count, group * heads, extent)
    mixture = blocks.transpose(1, 0, 2).reshape(share, width).astype(f32)
    layer_out = (hidden.astype(f32) + mixture).astype(bf16)
    return (layer_out, migrated)


def solution(mesh):
    return jax.shard_map(
        functools.partial(shards, mesh.shape["row"], mesh.shape["col"]),
        mesh=mesh,
        in_specs=(
            P(("row", "col"), None),
            P("row", "col"),
            P(None, "row", "col"),
            P(None, "row", "col", None),
            P("row", None),
            P("row"),
            P("col", None),
            P(),
            P(None, "row", "col"),
            P(None, "row", "col"),
            P(None, "col", "row"),
            P("row", None),
            P("row", None),
            P(None, "row", "col", None),
            P(None, "row"),
            P(),
        ),
        out_specs=(P(("row", "col"), None), P(None, "col", None, "row", None)),
        check_vma=False,
    )
```

```python
import functools
import math

import jax
import jax.numpy as jnp
from jax import lax
from jax.experimental import pallas as pl
from jax.experimental.pallas import tpu as pltpu
from jax.sharding import PartitionSpec as P

HD = 64
E = 8
TOP = 2
PAGE = 128
MAXP = 32
SPAN = 256
CAP = 128
WIN = CAP + 16

masked_score = -1e30
norm_eps = 1e-05
MESH = pl.DeviceIdType.MESH
f32 = jnp.float32
bf16 = jnp.bfloat16


QB = 128
STEP = 8
PAIRS = PAGE // 2

def make_plan(routes, weights):
    tokens = routes.shape[0]
    experts = lax.broadcasted_iota(jnp.int32, (tokens, E), 1)
    named = [routes[:, k : k + 1] == experts for k in range(TOP)]
    member = functools.reduce(jnp.logical_or, named).astype(f32).astype(bf16)
    scaled = sum(jnp.where(named[k], weights[:, k : k + 1], 0.0) for k in range(TOP)).astype(bf16)
    first = lax.broadcasted_iota(jnp.int32, (tokens, tokens), 0)
    second = lax.broadcasted_iota(jnp.int32, (tokens, tokens), 1)
    before = (first < second).astype(f32).astype(bf16)
    same = (first == second).astype(f32).astype(bf16)
    dims = (((0,), (0,)), ((), ()))
    rank = lax.dot_general(member, before, dims, preferred_element_type=f32)
    is_member = lax.dot_general(member, same, dims, preferred_element_type=f32)
    by_expert = lax.dot_general(scaled, same, dims, preferred_element_type=f32)
    lower = (
        lax.broadcasted_iota(jnp.int32, (E, E), 0) > lax.broadcasted_iota(jnp.int32, (E, E), 1)
    ).astype(f32).astype(bf16)
    ahead = jnp.dot(lower, is_member.astype(bf16), preferred_element_type=f32)
    offsets = jnp.sum(ahead, axis=1, keepdims=True)
    starts = jnp.minimum(jnp.floor(offsets * (1.0 / 16)) * 16.0, tokens * TOP - WIN)
    ranks = jnp.where(is_member > 0.5, rank + (offsets - starts), -1.0)
    return jnp.concatenate(
        [
            ranks,
            by_expert,
            jnp.broadcast_to(starts, ranks.shape),
            jnp.broadcast_to(offsets, ranks.shape),
        ],
        axis=0,
    )


def attend_body(
    ctx_ref, table_ref, ftable_ref, fdest_ref, q_ref, fresh_ref, weight_ref, routes_ref,
    route_weight_ref, cache_ref, pool_ref, part_ref, pages_ref, plan_ref,
    raw, picked, flat, heads_buf, out_buf, raw_sems, page_sem,
):
    head_count = cache_ref.shape[2]
    per = 8 // head_count
    finished, blocks = ftable_ref.shape

    def fetch(j, carry):
        page = table_ref[0, j]
        for kv in range(2):
            pltpu.make_async_copy(
                cache_ref.at[kv, page], raw.at[kv, j], raw_sems.at[kv, lax.div(j, STEP)]
            ).start()
        return carry

    lax.fori_loop(0, MAXP, fetch, 0, unroll=STEP)

    def regroup(f, carry):
        dest = fdest_ref[f]
        for kv in range(2):
            for b in range(blocks):
                pltpu.make_async_copy(
                    pool_ref.at[kv, ftable_ref[f, b]], picked.at[dest, kv, b], page_sem
                ).start()
        return carry

    lax.fori_loop(0, finished, regroup, 0)

    plan_ref[...] = make_plan(routes_ref[...], route_weight_ref[...])

    def spread(kv, first):
        for i in range(per):
            page = raw[kv, first + i].astype(f32)
            for t in range(PAIRS):
                flat[pl.ds(8 * t + i * head_count, head_count), :] = page[:, t * 128 : (t + 1) * 128]
        for i in range(per):
            for h in range(head_count):
                rows = flat[pl.ds(i * head_count + h, PAIRS, stride=8), :]
                where = pl.ds(pl.multiple_of((first + i) * PAIRS, PAIRS), PAIRS)
                heads_buf[kv, h, where, :] = rows.astype(bf16)

    for chunk in range(MAXP // STEP):
        for kv in range(2):
            pltpu.make_async_copy(
                raw.at[kv, pl.ds(chunk * STEP, STEP)],
                raw.at[kv, pl.ds(chunk * STEP, STEP)],
                raw_sems.at[kv, chunk],
            ).wait()

            @pl.loop(0, STEP // per)
            def _(g):
                spread(kv, chunk * STEP + g * per)

    pltpu.make_async_copy(picked, picked, page_sem).wait()
    to_pages = pltpu.make_async_copy(picked, pages_ref, page_sem)
    to_pages.start()
    context = ctx_ref[0]
    cached = MAXP * PAIRS
    scale = 1.0 / math.sqrt(HD)
    lanes = lax.broadcasted_iota(jnp.int32, (QB, 128), 1)
    low = lanes < HD
    column = lax.broadcasted_iota(jnp.int32, (QB, cached), 1)
    keep = [2 * column + p < context for p in range(2)]
    for block in range(SPAN // QB):
        rows = pl.ds(block * QB, QB)
        causal = (
            block * QB + lax.broadcasted_iota(jnp.int32, (QB, SPAN), 0)
            >= lax.broadcasted_iota(jnp.int32, (QB, SPAN), 1)
        )

        for pair in range((head_count + 1) // 2):
            lane = pl.ds(pair * 128, 128)
            both = q_ref[rows, lane].astype(f32) * scale
            turned = pltpu.roll(both, HD, 1)
            made = []
            for side in range(min(2, head_count - 2 * pair)):
                h = pair * 2 + side
                own = low if side == 0 else jnp.logical_not(low)
                straight = jnp.where(own, both, 0.0).astype(bf16)
                swapped = jnp.where(own, 0.0, turned).astype(bf16)
                by_parity = (straight, swapped) if side == 0 else (swapped, straight)
                keys = heads_buf[0, h]
                values = heads_buf[1, h]
                dims = (((1,), (1,)), ((), ()))
                s = [
                    jnp.where(
                        keep[p],
                        lax.dot_general(by_parity[p], keys, dims, preferred_element_type=f32),
                        masked_score,
                    )
                    for p in range(2)
                ]
                s_new = jnp.where(
                    causal,
                    lax.dot_general(straight, fresh_ref[0, :, lane], dims, preferred_element_type=f32),
                    masked_score,
                )
                highest = jnp.maximum(
                    jnp.max(jnp.maximum(s[0], s[1]), axis=1, keepdims=True),
                    jnp.max(s_new, axis=1, keepdims=True),
                )
                e = [jnp.exp(v - highest) for v in s]
                e_new = jnp.exp(s_new - highest)
                total = jnp.sum(e[0] + e[1], axis=1, keepdims=True) + jnp.sum(
                    e_new, axis=1, keepdims=True
                )
                o = [
                    jnp.dot(e[p].astype(bf16), values, preferred_element_type=f32)
                    for p in range(2)
                ]
                o_new = jnp.dot(
                    e_new.astype(bf16), fresh_ref[1, :, lane], preferred_element_type=f32
                )
                if side == 0:
                    o_cached = o[0] + pltpu.roll(o[1], HD, 1)
                else:
                    o_cached = o[1] + pltpu.roll(o[0], HD, 1)
                made.append((o_cached + o_new) / total)
            out_buf[rows, lane] = jnp.where(low, made[0], made[-1]).astype(bf16)
    part_ref[...] = jnp.dot(out_buf[...], weight_ref[...], preferred_element_type=f32).astype(bf16)
    to_pages.wait()


def attend(
    queries, fresh_cache, cache_pool, page_table, context, out_weight, routes, route_weight,
    finished_pool, finished_table, finished_dest,
):
    head_count = cache_pool.shape[2]
    extent = cache_pool.shape[3]
    finished, blocks = finished_table.shape
    odd = (head_count % 2) * HD
    queries = jnp.pad(queries, ((0, 0), (0, odd)))
    fresh_cache = jnp.pad(fresh_cache, ((0, 0), (0, 0), (0, odd)))
    out_weight = jnp.pad(out_weight, ((0, odd), (0, 0)))
    width = out_weight.shape[1]
    dma = pltpu.SemaphoreType.DMA
    vmem = pl.BlockSpec(memory_space=pltpu.VMEM)
    smem = pl.BlockSpec(memory_space=pltpu.SMEM)
    hbm = pl.BlockSpec(memory_space=pl.ANY)
    return pl.pallas_call(
        attend_body,
        out_shape=(
            jax.ShapeDtypeStruct((SPAN, width), bf16),
            jax.ShapeDtypeStruct((finished, 2, blocks, head_count, extent), bf16),
            jax.ShapeDtypeStruct((4 * E, SPAN), f32),
        ),
        in_specs=[smem] * 4 + [vmem] * 5 + [hbm] * 2,
        out_specs=(vmem, hbm, vmem),
        scratch_shapes=[
            pltpu.VMEM((2, MAXP, head_count, extent), bf16),
            pltpu.VMEM((finished, 2, blocks, head_count, extent), bf16),
            pltpu.VMEM((8 * PAIRS, 128), f32),
            pltpu.VMEM((2, head_count, MAXP * PAIRS, 128), bf16),
            pltpu.VMEM(queries.shape, bf16),
            dma((2, MAXP // STEP)), dma,
        ],
        compiler_params=pltpu.CompilerParams(vmem_limit_bytes=60 << 20),
    )(context, page_table, finished_table, finished_dest, queries, fresh_cache, out_weight,
      routes, route_weight, cache_pool, finished_pool)


def remote(src, dst, sems, index, where):
    copy = pltpu.make_async_remote_copy(
        src_ref=src,
        dst_ref=dst,
        send_sem=sems.at[0, index],
        recv_sem=sems.at[1, index],
        device_id=where,
        device_id_type=MESH,
    )
    copy.start()
    return copy


def greet(rows, cols):
    row, col = lax.axis_index("row"), lax.axis_index("col")
    a, b = col // 2, col % 2
    mate = {"col": a * 2 + (1 - b)}
    line = [{"col": lax.rem(a + 1 + s, cols // 2) * 2 + b} for s in range(cols // 2 - 1)]
    column = [{"row": lax.rem(row + 1 + s, rows)} for s in range(rows - 1)]
    barrier = pltpu.get_barrier_semaphore()
    peers = [mate] + line + column
    for peer in peers:
        pl.semaphore_signal(barrier, inc=1, device_id=peer, device_id_type=MESH)
    pl.semaphore_wait(barrier, len(peers))
    return row, col, mate, line, column


def start_mates(cols, block, mate_buf, mate_sems, mate):
    col = lax.axis_index("col")
    a, b = col // 2, col % 2
    return [
        remote(
            block(lax.rem(a + 1 + s, cols // 2) * 2 + (1 - b)), mate_buf.at[s], mate_sems, s, mate
        )
        for s in range(cols // 2)
    ]


def sum_cols(cols, load, to_mate, mate_buf, pair_buf, far_buf, far_sems, line):
    col = lax.axis_index("col")
    a, b = col // 2, col % 2
    half = cols // 2
    to_far = []
    for s in range(half - 1):
        to_mate[s].wait_recv()
        mine = load(lax.rem(a + 1 + s, half) * 2 + b)
        pair_buf[s] = (mine.astype(f32) + mate_buf[s].astype(f32)).astype(bf16)
        to_far.append(remote(pair_buf.at[s], far_buf.at[s], far_sems, s, line[s]))
    to_mate[half - 1].wait_recv()
    total = load(col).astype(f32) + mate_buf[half - 1].astype(f32)
    for s in range(half - 1):
        to_far[s].wait_recv()
        total = total + far_buf[s].astype(f32)
    return total, to_far


def hidden_body(
    rows, cols, part_ref, res_ref, gain_ref, plan_ref, hidden_ref, tokens_ref, plans_ref,
    mate_buf, pair_buf, far_buf, norm_buf,
    mate_sems, far_sems, row_sems, line_sems, pass_sems, plan_sems,
):
    half = cols // 2
    depth = tokens_ref.shape[3]
    row, col, mate, line, column = greet(rows, cols)
    a, b = col // 2, col % 2
    copies = start_mates(cols, lambda i: part_ref.at[i], mate_buf, mate_sems, mate)
    to_mate = list(copies)
    plans = [
        remote(plan_ref, plans_ref.at[row], plan_sems, s, column[s]) for s in range(rows - 1)
    ]
    plans_ref[row] = plan_ref[...]
    total, to_far = sum_cols(
        cols, lambda i: part_ref[i], to_mate, mate_buf, pair_buf, far_buf, far_sems, line
    )
    hidden = (res_ref[...].astype(f32) + total).astype(bf16)
    hidden_ref[...] = hidden
    values = hidden.astype(f32)
    meansq = jnp.mean(values * values, axis=-1, keepdims=True)
    normed = (values * lax.rsqrt(meansq + norm_eps) * gain_ref[...].astype(f32)).astype(bf16)
    for r in range(rows):
        norm_buf[r] = normed[:, r * depth : (r + 1) * depth]
    to_row = [
        remote(norm_buf.at[column[s]["row"]], tokens_ref.at[row, col], row_sems, s, column[s])
        for s in range(rows - 1)
    ]
    tokens_ref[row, col] = norm_buf[row]
    for copy in to_row:
        copy.wait_recv()
    block = tokens_ref.at[:, col]
    to_line = [remote(block, block, line_sems, s, line[s]) for s in range(half - 1)]
    passed = [remote(block, block, pass_sems, half - 1, mate)]
    for s in range(half - 1):
        to_line[s].wait_recv()
        origin = lax.rem(a - 1 - s + half, half) * 2 + b
        piece = tokens_ref.at[:, origin]
        passed.append(remote(piece, piece, pass_sems, s, mate))
    for copy in passed:
        copy.wait_recv()
    for copy in plans:
        copy.wait_recv()
    for copy in to_mate + plans + to_far + to_row + to_line + passed:
        copy.wait_send()


def make_hidden(rows, cols, part, residual, gain, plan, collective_id):
    share, width = residual.shape
    depth = width // rows
    half = cols // 2
    dma = pltpu.SemaphoreType.DMA
    vmem = pl.BlockSpec(memory_space=pltpu.VMEM)
    return pl.pallas_call(
        functools.partial(hidden_body, rows, cols),
        out_shape=(
            jax.ShapeDtypeStruct((share, width), bf16),
            jax.ShapeDtypeStruct((rows, cols, share, depth), bf16),
            jax.ShapeDtypeStruct((rows,) + plan.shape, f32),
        ),
        in_specs=[vmem] * 4,
        out_specs=(vmem, vmem, vmem),
        scratch_shapes=[
            pltpu.VMEM((half, share, width), bf16),
            pltpu.VMEM((half - 1, share, width), bf16),
            pltpu.VMEM((half - 1, share, width), bf16),
            pltpu.VMEM((rows, share, depth), bf16),
            dma((2, half)), dma((2, half)), dma((2, rows)), dma((2, half)), dma((2, half)),
            dma((2, rows)),
        ],
        compiler_params=pltpu.CompilerParams(
            collective_id=collective_id, has_side_effects=True, vmem_limit_bytes=32 << 20
        ),
    )(part, residual, gain, plan)


def gate_up_body(start_ref, plan_ref, x_ref, gate_ref, up_ref, out_ref, rows_ref):
    e = pl.program_id(0)
    groups, tokens = x_ref.shape[0], x_ref.shape[1]

    @pl.when(e == 0)
    def _():
        out_ref[...] = jnp.zeros_like(out_ref)

    slots = lax.broadcasted_iota(jnp.int32, (WIN, tokens), 0).astype(f32)
    for r in range(groups):
        pick = (slots == plan_ref[r, pl.ds(e, 1), :]).astype(f32).astype(bf16)
        rows_ref[r * WIN : (r + 1) * WIN, :] = jnp.dot(
            pick, x_ref[r], preferred_element_type=f32
        ).astype(bf16)
    for side, weight in enumerate((gate_ref, up_ref)):
        sums = jnp.dot(rows_ref[...], weight[0], preferred_element_type=f32).astype(bf16)
        for r in range(groups):
            window = pl.ds(pl.multiple_of(start_ref[r * E + e], 16), WIN)
            out_ref[r, side, window, :] += sums[r * WIN : (r + 1) * WIN]


def gate_up(starts, plans, x, w_gate, w_up):
    groups, tokens, depth = x.shape
    width = w_gate.shape[2]
    weight_spec = pl.BlockSpec((1, depth, width), lambda e, s: (e, 0, 0))
    return pl.pallas_call(
        gate_up_body,
        grid_spec=pltpu.PrefetchScalarGridSpec(
            num_scalar_prefetch=1,
            grid=(E,),
            in_specs=[
                pl.BlockSpec(plans.shape, lambda e, s: (0, 0, 0)),
                pl.BlockSpec((groups, tokens, depth), lambda e, s: (0, 0, 0)),
                weight_spec,
                weight_spec,
            ],
            out_specs=pl.BlockSpec((groups, 2, tokens * TOP, width), lambda e, s: (0, 0, 0, 0)),
            scratch_shapes=[pltpu.VMEM((groups * WIN, depth), bf16)],
        ),
        out_shape=jax.ShapeDtypeStruct((groups, 2, tokens * TOP, width), bf16),
        compiler_params=pltpu.CompilerParams(vmem_limit_bytes=44 << 20),
    )(starts, plans, x, w_gate, w_up)


CHUNKS = 4


def experts_body(
    rows, cols, plan_ref, part_ref, pages_ref, down_ref,
    out_ref, moved_ref,
    weights, near, far_act, mate_buf, far_out, far_buf, arrived, rows_buf, outs_buf, mix_buf,
    mixed, x_buf, pair_buf, z_buf, sum_buf,
    mate_sems, far_sems, near_sems, far_act_sems, pass_sems, col_sems, row_page_sems,
    x_sems, z_sems, row_sems, weight_sem,
):
    row, col = lax.axis_index("row"), lax.axis_index("col")
    y, core = row // 2, row % 2
    mate, far, diag = y * 2 + (1 - core), (1 - y) * 2 + core, (1 - y) * 2 + (1 - core)
    half = cols // 2
    group = cols // rows
    a, b = col // 2, col % 2
    x_mate = {"col": a * 2 + (1 - b)}
    line = [{"col": lax.rem(a + 1 + s, half) * 2 + b} for s in range(half - 1)]
    column = [{"row": r} for r in (mate, far, diag)]
    others = [lax.rem(col + 1 + s, cols) for s in range(cols - 1)]
    height = part_ref.shape[2] // CHUNKS
    share, depth = out_ref.shape[1], out_ref.shape[2]

    to_weights = pltpu.make_async_copy(down_ref, weights, weight_sem)
    to_weights.start()
    barrier = pltpu.get_barrier_semaphore()
    peers = column + [{"col": c} for c in others]
    for peer in peers:
        pl.semaphore_signal(barrier, inc=1, device_id=peer, device_id_type=MESH)
    pl.semaphore_wait(barrier, len(peers))
    sent = []

    def send(src, dst, sems, index, where):
        copy = remote(src, dst, sems, index, where)
        sent.append(copy)
        return copy

    def chunk(k):
        return pl.ds(k * height, height)

    to_mate = [[], []]
    for which, side in ((0, 1 - y), (1, y)):
        for k in range(CHUNKS):
            to_mate[which].append(
                send(
                    part_ref.at[side * 2 + (1 - core), :, chunk(k)],
                    mate_buf.at[which, :, chunk(k)],
                    mate_sems, which * CHUNKS + k, column[0],
                )
            )
    pages = [
        send(pages_ref.at[c], arrived.at[col], col_sems, s, {"col": c})
        for s, c in enumerate(others)
    ]
    arrived[col] = pages_ref[col]
    to_far = []
    for k in range(CHUNKS):
        to_mate[0][k].wait_recv()
        far_out[:, chunk(k), :] = (
            part_ref[far, :, chunk(k), :].astype(f32) + mate_buf[0, :, chunk(k), :].astype(f32)
        ).astype(bf16)
        to_far.append(
            send(far_out.at[:, chunk(k)], far_buf.at[:, chunk(k)], far_sems, k, column[1])
        )
    to_near, to_far_act = [], []
    for k in range(CHUNKS):
        to_mate[1][k].wait_recv()
        to_far[k].wait_recv()
        sums = [
            part_ref[row, s, chunk(k), :].astype(f32)
            + mate_buf[1, s, chunk(k), :].astype(f32)
            + far_buf[s, chunk(k), :].astype(f32)
            for s in range(2)
        ]
        near[core, chunk(k), :] = (sums[0] / (1.0 + jnp.exp(-sums[0])) * sums[1]).astype(bf16)
        block = near.at[core, chunk(k)]
        to_far_act.append(send(block, far_act.at[core, chunk(k)], far_act_sems, k, column[1]))
        to_near.append(send(block, near.at[core, chunk(k)], near_sems, k, column[0]))

    pairs, tokens = near.shape[1], mix_buf.shape[2]
    slots = lax.broadcasted_iota(jnp.int32, (CAP, tokens), 0).astype(f32)
    ahead = (
        lax.broadcasted_iota(jnp.int32, (CAP, pairs), 1)
        - lax.broadcasted_iota(jnp.int32, (CAP, pairs), 0)
    ).astype(f32)

    def down(batch, act, side):
        @pl.loop(0, E)
        def _(e):
            for c in range(2):
                offset = plan_ref[side * 2 + c, pl.ds(3 * E + e, 1), :]
                offset = jnp.concatenate([offset] * TOP, axis=1)
                pick = (ahead == offset).astype(f32).astype(bf16)
                rows_buf[c * CAP : (c + 1) * CAP, :] = jnp.dot(
                    pick, act[c], preferred_element_type=f32
                ).astype(bf16)
            outs = lax.dot_general(
                rows_buf[...], weights[e], (((1,), (1,)), ((), ())), preferred_element_type=f32
            ).astype(bf16)
            place = pl.ds(pl.multiple_of(e * CAP, CAP), CAP)
            for c in range(2):
                r = side * 2 + c
                outs_buf[c, place, :] = outs[c * CAP : (c + 1) * CAP]
                shift = (
                    plan_ref[r, pl.ds(3 * E + e, 1), :] - plan_ref[r, pl.ds(2 * E + e, 1), :]
                )
                mix_buf[c, place, :] = jnp.where(
                    slots == plan_ref[r, pl.ds(e, 1), :] - shift,
                    plan_ref[r, pl.ds(E + e, 1), :],
                    0.0,
                ).astype(bf16)

        for c in range(2):
            total = lax.dot_general(
                mix_buf[c], outs_buf[c], (((0,), (0,)), ((), ())), preferred_element_type=f32
            ).astype(bf16)
            mixed[batch, c] = total.reshape(cols, share, depth)

    def start_x(batch):
        return [
            send(
                mixed.at[batch, :, lax.rem(a + 1 + s, half) * 2 + (1 - b)],
                x_buf.at[batch, s], x_sems, batch * half + s, x_mate,
            )
            for s in range(half)
        ]

    def start_z(batch, to_x):
        to_z = []
        for s in range(half - 1):
            to_x[s].wait_recv()
            mine = mixed[batch, :, lax.rem(a + 1 + s, half) * 2 + b]
            pair_buf[batch, s] = (mine.astype(f32) + x_buf[batch, s].astype(f32)).astype(bf16)
            to_z.append(
                send(
                    pair_buf.at[batch, s], z_buf.at[batch, s],
                    z_sems, batch * half + s, line[s],
                )
            )
        return to_z

    def finish(batch, to_x, to_z):
        to_x[half - 1].wait_recv()
        total = mixed[batch, :, col].astype(f32) + x_buf[batch, half - 1].astype(f32)
        for s in range(half - 1):
            to_z[s].wait_recv()
            total = total + z_buf[batch, s].astype(f32)
        sum_buf[batch] = total.astype(bf16)

    to_weights.wait()
    for k in range(CHUNKS):
        to_near[k].wait_recv()
    down(0, near, y)
    near_x = start_x(0)
    near_z = start_z(0, near_x)
    passed = []
    for k in range(CHUNKS):
        to_far_act[k].wait_recv()
        block = far_act.at[core, chunk(k)]
        passed.append(send(block, block, pass_sems, k, column[0]))
    for copy in passed:
        copy.wait_recv()
    down(1, far_act, 1 - y)
    far_x = start_x(1)
    for copy in pages:
        copy.wait_recv()
    row_pages = [
        send(
            arrived.at[pl.ds(column[s]["row"] * group, group)],
            moved_ref.at[row], row_page_sems, s, column[s],
        )
        for s in range(rows - 1)
    ]
    finish(0, near_x, near_z)
    to_row = [send(sum_buf.at[0, 1 - core], out_ref.at[row], row_sems, 0, column[0])]
    out_ref[row] = sum_buf[0, core]
    far_z = start_z(1, far_x)
    for i in range(group):
        moved_ref[row, i] = arrived[row * group + i]
    finish(1, far_x, far_z)
    to_row.append(send(sum_buf.at[1, core], out_ref.at[row], row_sems, 1, column[1]))
    to_row.append(send(sum_buf.at[1, 1 - core], out_ref.at[row], row_sems, 2, column[2]))
    for copy in to_row + row_pages:
        copy.wait_recv()
    for copy in sent:
        copy.wait_send()


def run_experts(rows, cols, plans, part, pages, w_down, collective_id):
    groups, _, pairs, width = part.shape
    tokens = pairs // TOP
    depth = w_down.shape[2]
    share = tokens // cols
    half = cols // 2
    w_down = w_down.transpose(0, 2, 1)
    dma = pltpu.SemaphoreType.DMA
    vmem = pl.BlockSpec(memory_space=pltpu.VMEM)
    block = (groups // 2, share, depth)
    return pl.pallas_call(
        functools.partial(experts_body, rows, cols),
        out_shape=(
            jax.ShapeDtypeStruct((rows, share, depth), bf16),
            jax.ShapeDtypeStruct((rows, cols // rows) + pages.shape[1:], bf16),
        ),
        in_specs=[
            vmem, vmem, vmem, pl.BlockSpec(memory_space=pl.ANY),
        ],
        out_specs=(vmem, vmem),
        scratch_shapes=[
            pltpu.VMEM(w_down.shape, bf16),
            pltpu.VMEM((2, pairs, width), bf16),
            pltpu.VMEM((2, pairs, width), bf16),
            pltpu.VMEM((2, 2, pairs, width), bf16),
            pltpu.VMEM((2, pairs, width), bf16),
            pltpu.VMEM((2, pairs, width), bf16),
            pltpu.VMEM(pages.shape, bf16),
            pltpu.VMEM((2 * CAP, width), bf16),
            pltpu.VMEM((2, E * CAP, depth), bf16),
            pltpu.VMEM((2, E * CAP, tokens), bf16),
            pltpu.VMEM((2, groups // 2, cols, share, depth), bf16),
            pltpu.VMEM((2, half) + block, bf16),
            pltpu.VMEM((2, half - 1) + block, bf16),
            pltpu.VMEM((2, half - 1) + block, bf16),
            pltpu.VMEM((2,) + block, bf16),
            dma((2, 2 * CHUNKS)), dma((2, CHUNKS)), dma((2, CHUNKS)), dma((2, CHUNKS)),
            dma((2, CHUNKS)), dma((2, cols)), dma((2, rows)),
            dma((2, 2 * half)), dma((2, 2 * half)), dma((2, rows)), dma,
        ],
        compiler_params=pltpu.CompilerParams(
            collective_id=collective_id, has_side_effects=True, vmem_limit_bytes=56 << 20
        ),
    )(plans, part, pages, w_down)


def shards(
    row_count,
    col_count,
    residual_in,
    queries,
    fresh_cache,
    cache_pool,
    page_table,
    context,
    out_weight,
    norm_gain,
    w_gate,
    w_up,
    w_down,
    routes,
    route_weight,
    finished_pool,
    finished_table,
    finished_dest,
):
    share, width = residual_in.shape
    depth = width // row_count
    partial_value, picked, plan = attend(
        queries, fresh_cache, cache_pool, page_table, context, out_weight, routes, route_weight,
        finished_pool, finished_table, finished_dest,
    )
    hidden, tokens, plans = make_hidden(
        row_count,
        col_count,
        partial_value.reshape(col_count, share, width),
        residual_in,
        norm_gain.reshape(1, width),
        plan,
        0,
    )
    starts = plans[:, 2 * E : 3 * E, 0].astype(jnp.int32).reshape(-1)
    tokens = tokens.reshape(row_count, col_count * share, depth)
    part = gate_up(starts, plans, tokens, w_gate, w_up)
    pages = picked.reshape((col_count, picked.shape[0] // col_count) + picked.shape[1:])
    blocks, moved = run_experts(
        row_count, col_count, plans, part, pages, w_down, 1
    )
    _, group, requests, sides, block_count, heads, extent = moved.shape
    migrated = moved.transpose(3, 2, 0, 4, 1, 5, 6)
    migrated = migrated.reshape(sides, requests, row_count * block_count, group * heads, extent)
    mixture = blocks.transpose(1, 0, 2).reshape(share, width).astype(f32)
    layer_out = (hidden.astype(f32) + mixture).astype(bf16)
    return (layer_out, migrated)


def solution(mesh):
    return jax.shard_map(
        functools.partial(shards, mesh.shape["row"], mesh.shape["col"]),
        mesh=mesh,
        in_specs=(
            P(("row", "col"), None),
            P("row", "col"),
            P(None, "row", "col"),
            P(None, "row", "col", None),
            P("row", None),
            P("row"),
            P("col", None),
            P(),
            P(None, "row", "col"),
            P(None, "row", "col"),
            P(None, "col", "row"),
            P("row", None),
            P("row", None),
            P(None, "row", "col", None),
            P(None, "row"),
            P(),
        ),
        out_specs=(P(("row", "col"), None), P(None, "col", None, "row", None)),
        check_vma=False,
    )
```

```python
import functools
import math

import jax
import jax.numpy as jnp
from jax import lax
from jax.experimental import pallas as pl
from jax.experimental.pallas import tpu as pltpu
from jax.sharding import PartitionSpec as P

HD = 64
E = 8
TOP = 2
PAGE = 128
MAXP = 32
SPAN = 256
CAP = 128
WIN = CAP + 16

masked_score = -1e30
norm_eps = 1e-05
MESH = pl.DeviceIdType.MESH
f32 = jnp.float32
bf16 = jnp.bfloat16


QB = 128
STEP = 8
PAIRS = PAGE // 2

def make_plan(routes, weights):
    tokens = routes.shape[1]
    experts = lax.broadcasted_iota(jnp.int32, (E, tokens), 0)
    named = [routes[k : k + 1, :] == experts for k in range(TOP)]
    is_member = functools.reduce(jnp.logical_or, named)
    member = is_member.astype(f32).astype(bf16)
    by_expert = sum(jnp.where(named[k], weights[k : k + 1, :], 0.0) for k in range(TOP))
    before = (
        lax.broadcasted_iota(jnp.int32, (tokens, tokens), 0)
        < lax.broadcasted_iota(jnp.int32, (tokens, tokens), 1)
    ).astype(f32).astype(bf16)
    rank = jnp.dot(member, before, preferred_element_type=f32)
    lower = (
        lax.broadcasted_iota(jnp.int32, (E, E), 0) > lax.broadcasted_iota(jnp.int32, (E, E), 1)
    ).astype(f32).astype(bf16)
    ahead = jnp.dot(lower, member, preferred_element_type=f32)
    offsets = jnp.sum(ahead, axis=1, keepdims=True)
    starts = jnp.minimum(jnp.floor(offsets * (1.0 / 16)) * 16.0, tokens * TOP - WIN)
    ranks = jnp.where(is_member, rank + (offsets - starts), -1.0)
    return jnp.concatenate(
        [
            ranks,
            by_expert,
            jnp.broadcast_to(starts, ranks.shape),
            jnp.broadcast_to(offsets, ranks.shape),
        ],
        axis=0,
    )


def attend_body(
    ctx_ref, table_ref, ftable_ref, fdest_ref, q_ref, fresh_ref, weight_ref, routes_ref,
    route_weight_ref, cache_ref, pool_ref, part_ref, pages_ref, plan_ref,
    raw, picked, flat, heads_buf, out_buf, raw_sems, page_sem,
):
    head_count = cache_ref.shape[2]
    per = 8 // head_count
    blocks, finished = ftable_ref.shape

    def fetch(j, carry):
        page = table_ref[0, j]
        for kv in range(2):
            pltpu.make_async_copy(
                cache_ref.at[kv, page], raw.at[kv, j], raw_sems.at[kv, lax.div(j, STEP)]
            ).start()
        return carry

    lax.fori_loop(0, MAXP, fetch, 0, unroll=STEP)

    def regroup(f, carry):
        dest = fdest_ref[f]
        for kv in range(2):
            for b in range(blocks):
                pltpu.make_async_copy(
                    pool_ref.at[kv, ftable_ref[b, f]], picked.at[dest, kv, b], page_sem
                ).start()
        return carry

    lax.fori_loop(0, finished, regroup, 0)

    plan_ref[...] = make_plan(routes_ref[...], route_weight_ref[...])

    def spread(kv, first):
        for i in range(per):
            page = raw[kv, first + i].astype(f32)
            for t in range(PAIRS):
                flat[pl.ds(8 * t + i * head_count, head_count), :] = page[:, t * 128 : (t + 1) * 128]
        for i in range(per):
            for h in range(head_count):
                rows = flat[pl.ds(i * head_count + h, PAIRS, stride=8), :]
                where = pl.ds(pl.multiple_of((first + i) * PAIRS, PAIRS), PAIRS)
                heads_buf[kv, h, where, :] = rows.astype(bf16)

    for chunk in range(MAXP // STEP):
        for kv in range(2):
            pltpu.make_async_copy(
                raw.at[kv, pl.ds(chunk * STEP, STEP)],
                raw.at[kv, pl.ds(chunk * STEP, STEP)],
                raw_sems.at[kv, chunk],
            ).wait()

            @pl.loop(0, STEP // per)
            def _(g):
                spread(kv, chunk * STEP + g * per)

    pltpu.make_async_copy(picked, picked, page_sem).wait()
    to_pages = pltpu.make_async_copy(picked, pages_ref, page_sem)
    to_pages.start()
    context = ctx_ref[0]
    cached = MAXP * PAIRS
    scale = 1.0 / math.sqrt(HD)
    lanes = lax.broadcasted_iota(jnp.int32, (QB, 128), 1)
    low = lanes < HD
    column = lax.broadcasted_iota(jnp.int32, (QB, cached), 1)
    keep = [2 * column + p < context for p in range(2)]
    for block in range(SPAN // QB):
        rows = pl.ds(block * QB, QB)
        causal = (
            block * QB + lax.broadcasted_iota(jnp.int32, (QB, SPAN), 0)
            >= lax.broadcasted_iota(jnp.int32, (QB, SPAN), 1)
        )

        for pair in range((head_count + 1) // 2):
            lane = pl.ds(pair * 128, 128)
            both = q_ref[rows, lane].astype(f32) * scale
            turned = pltpu.roll(both, HD, 1)
            made = []
            for side in range(min(2, head_count - 2 * pair)):
                h = pair * 2 + side
                own = low if side == 0 else jnp.logical_not(low)
                straight = jnp.where(own, both, 0.0).astype(bf16)
                swapped = jnp.where(own, 0.0, turned).astype(bf16)
                by_parity = (straight, swapped) if side == 0 else (swapped, straight)
                keys = heads_buf[0, h]
                values = heads_buf[1, h]
                dims = (((1,), (1,)), ((), ()))
                s = [
                    jnp.where(
                        keep[p],
                        lax.dot_general(by_parity[p], keys, dims, preferred_element_type=f32),
                        masked_score,
                    )
                    for p in range(2)
                ]
                s_new = jnp.where(
                    causal,
                    lax.dot_general(straight, fresh_ref[0, :, lane], dims, preferred_element_type=f32),
                    masked_score,
                )
                highest = jnp.maximum(
                    jnp.max(jnp.maximum(s[0], s[1]), axis=1, keepdims=True),
                    jnp.max(s_new, axis=1, keepdims=True),
                )
                e = [jnp.exp(v - highest) for v in s]
                e_new = jnp.exp(s_new - highest)
                total = jnp.sum(e[0] + e[1], axis=1, keepdims=True) + jnp.sum(
                    e_new, axis=1, keepdims=True
                )
                o = [
                    jnp.dot(e[p].astype(bf16), values, preferred_element_type=f32)
                    for p in range(2)
                ]
                o_new = jnp.dot(
                    e_new.astype(bf16), fresh_ref[1, :, lane], preferred_element_type=f32
                )
                if side == 0:
                    o_cached = o[0] + pltpu.roll(o[1], HD, 1)
                else:
                    o_cached = o[1] + pltpu.roll(o[0], HD, 1)
                made.append((o_cached + o_new) / total)
            out_buf[rows, lane] = jnp.where(low, made[0], made[-1]).astype(bf16)
    part_ref[...] = jnp.dot(out_buf[...], weight_ref[...], preferred_element_type=f32).astype(bf16)
    to_pages.wait()


def attend(
    queries, fresh_cache, cache_pool, page_table, context, out_weight, routes, route_weight,
    finished_pool, finished_table, finished_dest,
):
    head_count = cache_pool.shape[2]
    extent = cache_pool.shape[3]
    finished, blocks = finished_table.shape
    odd = (head_count % 2) * HD
    queries = jnp.pad(queries, ((0, 0), (0, odd)))
    fresh_cache = jnp.pad(fresh_cache, ((0, 0), (0, 0), (0, odd)))
    out_weight = jnp.pad(out_weight, ((0, odd), (0, 0)))
    width = out_weight.shape[1]
    dma = pltpu.SemaphoreType.DMA
    vmem = pl.BlockSpec(memory_space=pltpu.VMEM)
    smem = pl.BlockSpec(memory_space=pltpu.SMEM)
    hbm = pl.BlockSpec(memory_space=pl.ANY)
    return pl.pallas_call(
        attend_body,
        out_shape=(
            jax.ShapeDtypeStruct((SPAN, width), bf16),
            jax.ShapeDtypeStruct((finished, 2, blocks, head_count, extent), bf16),
            jax.ShapeDtypeStruct((4 * E, SPAN), f32),
        ),
        in_specs=[smem] * 4 + [vmem] * 5 + [hbm] * 2,
        out_specs=(vmem, hbm, vmem),
        scratch_shapes=[
            pltpu.VMEM((2, MAXP, head_count, extent), bf16),
            pltpu.VMEM((finished, 2, blocks, head_count, extent), bf16),
            pltpu.VMEM((8 * PAIRS, 128), f32),
            pltpu.VMEM((2, head_count, MAXP * PAIRS, 128), bf16),
            pltpu.VMEM(queries.shape, bf16),
            dma((2, MAXP // STEP)), dma,
        ],
        compiler_params=pltpu.CompilerParams(vmem_limit_bytes=60 << 20),
    )(context, page_table, finished_table.T, finished_dest, queries, fresh_cache, out_weight,
      routes.T, route_weight.T, cache_pool, finished_pool)


def remote(src, dst, sems, index, where):
    copy = pltpu.make_async_remote_copy(
        src_ref=src,
        dst_ref=dst,
        send_sem=sems.at[0, index],
        recv_sem=sems.at[1, index],
        device_id=where,
        device_id_type=MESH,
    )
    copy.start()
    return copy


def greet(rows, cols):
    row, col = lax.axis_index("row"), lax.axis_index("col")
    a, b = col // 2, col % 2
    mate = {"col": a * 2 + (1 - b)}
    line = [{"col": lax.rem(a + 1 + s, cols // 2) * 2 + b} for s in range(cols // 2 - 1)]
    column = [{"row": lax.rem(row + 1 + s, rows)} for s in range(rows - 1)]
    barrier = pltpu.get_barrier_semaphore()
    peers = [mate] + line + column
    for peer in peers:
        pl.semaphore_signal(barrier, inc=1, device_id=peer, device_id_type=MESH)
    pl.semaphore_wait(barrier, len(peers))
    return row, col, mate, line, column


def start_mates(cols, block, mate_buf, mate_sems, mate):
    col = lax.axis_index("col")
    a, b = col // 2, col % 2
    return [
        remote(
            block(lax.rem(a + 1 + s, cols // 2) * 2 + (1 - b)), mate_buf.at[s], mate_sems, s, mate
        )
        for s in range(cols // 2)
    ]


def sum_cols(cols, load, to_mate, mate_buf, pair_buf, far_buf, far_sems, line):
    col = lax.axis_index("col")
    a, b = col // 2, col % 2
    half = cols // 2
    to_far = []
    for s in range(half - 1):
        to_mate[s].wait_recv()
        mine = load(lax.rem(a + 1 + s, half) * 2 + b)
        pair_buf[s] = (mine.astype(f32) + mate_buf[s].astype(f32)).astype(bf16)
        to_far.append(remote(pair_buf.at[s], far_buf.at[s], far_sems, s, line[s]))
    to_mate[half - 1].wait_recv()
    total = load(col).astype(f32) + mate_buf[half - 1].astype(f32)
    for s in range(half - 1):
        to_far[s].wait_recv()
        total = total + far_buf[s].astype(f32)
    return total, to_far


def hidden_body(
    rows, cols, part_ref, res_ref, gain_ref, plan_ref, hidden_ref, tokens_ref, plans_ref,
    mate_buf, pair_buf, far_buf, norm_buf,
    mate_sems, far_sems, row_sems, line_sems, pass_sems, plan_sems,
):
    half = cols // 2
    depth = tokens_ref.shape[3]
    row, col, mate, line, column = greet(rows, cols)
    a, b = col // 2, col % 2
    copies = start_mates(cols, lambda i: part_ref.at[i], mate_buf, mate_sems, mate)
    to_mate = list(copies)
    plans = [
        remote(plan_ref, plans_ref.at[row], plan_sems, s, column[s]) for s in range(rows - 1)
    ]
    plans_ref[row] = plan_ref[...]
    total, to_far = sum_cols(
        cols, lambda i: part_ref[i], to_mate, mate_buf, pair_buf, far_buf, far_sems, line
    )
    hidden = (res_ref[...].astype(f32) + total).astype(bf16)
    hidden_ref[...] = hidden
    values = hidden.astype(f32)
    meansq = jnp.mean(values * values, axis=-1, keepdims=True)
    normed = (values * lax.rsqrt(meansq + norm_eps) * gain_ref[...].astype(f32)).astype(bf16)
    for r in range(rows):
        norm_buf[r] = normed[:, r * depth : (r + 1) * depth]
    to_row = [
        remote(norm_buf.at[column[s]["row"]], tokens_ref.at[row, col], row_sems, s, column[s])
        for s in range(rows - 1)
    ]
    tokens_ref[row, col] = norm_buf[row]
    for copy in to_row:
        copy.wait_recv()
    block = tokens_ref.at[:, col]
    to_line = [remote(block, block, line_sems, s, line[s]) for s in range(half - 1)]
    passed = [remote(block, block, pass_sems, half - 1, mate)]
    for s in range(half - 1):
        to_line[s].wait_recv()
        origin = lax.rem(a - 1 - s + half, half) * 2 + b
        piece = tokens_ref.at[:, origin]
        passed.append(remote(piece, piece, pass_sems, s, mate))
    for copy in passed:
        copy.wait_recv()
    for copy in plans:
        copy.wait_recv()
    for copy in to_mate + plans + to_far + to_row + to_line + passed:
        copy.wait_send()


def make_hidden(rows, cols, part, residual, gain, plan, collective_id):
    share, width = residual.shape
    depth = width // rows
    half = cols // 2
    dma = pltpu.SemaphoreType.DMA
    vmem = pl.BlockSpec(memory_space=pltpu.VMEM)
    return pl.pallas_call(
        functools.partial(hidden_body, rows, cols),
        out_shape=(
            jax.ShapeDtypeStruct((share, width), bf16),
            jax.ShapeDtypeStruct((rows, cols, share, depth), bf16),
            jax.ShapeDtypeStruct((rows,) + plan.shape, f32),
        ),
        in_specs=[vmem] * 4,
        out_specs=(vmem, vmem, vmem),
        scratch_shapes=[
            pltpu.VMEM((half, share, width), bf16),
            pltpu.VMEM((half - 1, share, width), bf16),
            pltpu.VMEM((half - 1, share, width), bf16),
            pltpu.VMEM((rows, share, depth), bf16),
            dma((2, half)), dma((2, half)), dma((2, rows)), dma((2, half)), dma((2, half)),
            dma((2, rows)),
        ],
        compiler_params=pltpu.CompilerParams(
            collective_id=collective_id, has_side_effects=True, vmem_limit_bytes=32 << 20
        ),
    )(part, residual, gain, plan)


def gate_up_body(start_ref, plan_ref, x_ref, gate_ref, up_ref, out_ref, rows_ref):
    e = pl.program_id(0)
    groups, tokens = x_ref.shape[0], x_ref.shape[1]

    @pl.when(e == 0)
    def _():
        out_ref[...] = jnp.zeros_like(out_ref)

    slots = lax.broadcasted_iota(jnp.int32, (WIN, tokens), 0).astype(f32)
    for r in range(groups):
        pick = (slots == plan_ref[r, pl.ds(e, 1), :]).astype(f32).astype(bf16)
        rows_ref[r * WIN : (r + 1) * WIN, :] = jnp.dot(
            pick, x_ref[r], preferred_element_type=f32
        ).astype(bf16)
    for side, weight in enumerate((gate_ref, up_ref)):
        sums = jnp.dot(rows_ref[...], weight[0], preferred_element_type=f32).astype(bf16)
        for r in range(groups):
            window = pl.ds(pl.multiple_of(start_ref[r * E + e], 16), WIN)
            out_ref[r, side, window, :] += sums[r * WIN : (r + 1) * WIN]


def gate_up(starts, plans, x, w_gate, w_up):
    groups, tokens, depth = x.shape
    width = w_gate.shape[2]
    weight_spec = pl.BlockSpec((1, depth, width), lambda e, s: (e, 0, 0))
    return pl.pallas_call(
        gate_up_body,
        grid_spec=pltpu.PrefetchScalarGridSpec(
            num_scalar_prefetch=1,
            grid=(E,),
            in_specs=[
                pl.BlockSpec(plans.shape, lambda e, s: (0, 0, 0)),
                pl.BlockSpec((groups, tokens, depth), lambda e, s: (0, 0, 0)),
                weight_spec,
                weight_spec,
            ],
            out_specs=pl.BlockSpec((groups, 2, tokens * TOP, width), lambda e, s: (0, 0, 0, 0)),
            scratch_shapes=[pltpu.VMEM((groups * WIN, depth), bf16)],
        ),
        out_shape=jax.ShapeDtypeStruct((groups, 2, tokens * TOP, width), bf16),
        compiler_params=pltpu.CompilerParams(vmem_limit_bytes=44 << 20),
    )(starts, plans, x, w_gate, w_up)


CHUNKS = 4


def experts_body(
    rows, cols, plan_ref, part_ref, pages_ref, down_ref,
    out_ref, moved_ref,
    weights, near, far_act, mate_buf, far_out, far_buf, arrived, rows_buf, outs_buf, mix_buf,
    mixed, x_buf, pair_buf, z_buf, sum_buf,
    mate_sems, far_sems, near_sems, far_act_sems, pass_sems, col_sems, row_page_sems,
    x_sems, z_sems, row_sems, weight_sem,
):
    row, col = lax.axis_index("row"), lax.axis_index("col")
    y, core = row // 2, row % 2
    mate, far, diag = y * 2 + (1 - core), (1 - y) * 2 + core, (1 - y) * 2 + (1 - core)
    half = cols // 2
    group = cols // rows
    a, b = col // 2, col % 2
    x_mate = {"col": a * 2 + (1 - b)}
    line = [{"col": lax.rem(a + 1 + s, half) * 2 + b} for s in range(half - 1)]
    column = [{"row": r} for r in (mate, far, diag)]
    others = [lax.rem(col + 1 + s, cols) for s in range(cols - 1)]
    height = part_ref.shape[2] // CHUNKS
    share, depth = out_ref.shape[1], out_ref.shape[2]

    to_weights = pltpu.make_async_copy(down_ref, weights, weight_sem)
    to_weights.start()
    barrier = pltpu.get_barrier_semaphore()
    peers = column + [{"col": c} for c in others]
    for peer in peers:
        pl.semaphore_signal(barrier, inc=1, device_id=peer, device_id_type=MESH)
    pl.semaphore_wait(barrier, len(peers))
    sent = []

    def send(src, dst, sems, index, where):
        copy = remote(src, dst, sems, index, where)
        sent.append(copy)
        return copy

    def chunk(k):
        return pl.ds(k * height, height)

    def start_mate(which, side, k):
        return send(
            part_ref.at[side * 2 + (1 - core), :, chunk(k)],
            mate_buf.at[which, :, chunk(k)],
            mate_sems, which * CHUNKS + k, column[0],
        )

    to_mate = [[start_mate(0, 1 - y, k) for k in range(CHUNKS)], []]
    to_far = []
    for k in range(CHUNKS):
        to_mate[0][k].wait_recv()
        far_out[:, chunk(k), :] = (
            part_ref[far, :, chunk(k), :].astype(f32) + mate_buf[0, :, chunk(k), :].astype(f32)
        ).astype(bf16)
        to_far.append(
            send(far_out.at[:, chunk(k)], far_buf.at[:, chunk(k)], far_sems, k, column[1])
        )
        to_mate[1].append(start_mate(1, y, k))
    pages = [
        send(pages_ref.at[c], arrived.at[col], col_sems, s, {"col": c})
        for s, c in enumerate(others)
    ]
    arrived[col] = pages_ref[col]
    to_near, to_far_act = [], []
    for k in range(CHUNKS):
        to_mate[1][k].wait_recv()
        to_far[k].wait_recv()
        sums = [
            part_ref[row, s, chunk(k), :].astype(f32)
            + mate_buf[1, s, chunk(k), :].astype(f32)
            + far_buf[s, chunk(k), :].astype(f32)
            for s in range(2)
        ]
        near[core, chunk(k), :] = (sums[0] / (1.0 + jnp.exp(-sums[0])) * sums[1]).astype(bf16)
        block = near.at[core, chunk(k)]
        to_far_act.append(send(block, far_act.at[core, chunk(k)], far_act_sems, k, column[1]))
        to_near.append(send(block, near.at[core, chunk(k)], near_sems, k, column[0]))

    pairs, tokens = near.shape[1], mix_buf.shape[2]
    slots = lax.broadcasted_iota(jnp.int32, (CAP, tokens), 0).astype(f32)
    ahead = (
        lax.broadcasted_iota(jnp.int32, (CAP, pairs), 1)
        - lax.broadcasted_iota(jnp.int32, (CAP, pairs), 0)
    ).astype(f32)

    def down(batch, act, side):
        @pl.loop(0, E)
        def _(e):
            for c in range(2):
                offset = plan_ref[side * 2 + c, pl.ds(3 * E + e, 1), :]
                offset = jnp.concatenate([offset] * TOP, axis=1)
                pick = (ahead == offset).astype(f32).astype(bf16)
                rows_buf[c * CAP : (c + 1) * CAP, :] = jnp.dot(
                    pick, act[c], preferred_element_type=f32
                ).astype(bf16)
            outs = lax.dot_general(
                rows_buf[...], weights[e], (((1,), (1,)), ((), ())), preferred_element_type=f32
            ).astype(bf16)
            place = pl.ds(pl.multiple_of(e * CAP, CAP), CAP)
            for c in range(2):
                r = side * 2 + c
                outs_buf[c, place, :] = outs[c * CAP : (c + 1) * CAP]
                shift = (
                    plan_ref[r, pl.ds(3 * E + e, 1), :] - plan_ref[r, pl.ds(2 * E + e, 1), :]
                )
                mix_buf[c, place, :] = jnp.where(
                    slots == plan_ref[r, pl.ds(e, 1), :] - shift,
                    plan_ref[r, pl.ds(E + e, 1), :],
                    0.0,
                ).astype(bf16)

        for c in range(2):
            total = lax.dot_general(
                mix_buf[c], outs_buf[c], (((0,), (0,)), ((), ())), preferred_element_type=f32
            ).astype(bf16)
            mixed[batch, c] = total.reshape(cols, share, depth)

    def start_x(batch):
        return [
            send(
                mixed.at[batch, :, lax.rem(a + 1 + s, half) * 2 + (1 - b)],
                x_buf.at[batch, s], x_sems, batch * half + s, x_mate,
            )
            for s in range(half)
        ]

    def start_z(batch, to_x):
        to_z = []
        for s in range(half - 1):
            to_x[s].wait_recv()
            mine = mixed[batch, :, lax.rem(a + 1 + s, half) * 2 + b]
            pair_buf[batch, s] = (mine.astype(f32) + x_buf[batch, s].astype(f32)).astype(bf16)
            to_z.append(
                send(
                    pair_buf.at[batch, s], z_buf.at[batch, s],
                    z_sems, batch * half + s, line[s],
                )
            )
        return to_z

    def finish(batch, to_x, to_z):
        to_x[half - 1].wait_recv()
        total = mixed[batch, :, col].astype(f32) + x_buf[batch, half - 1].astype(f32)
        for s in range(half - 1):
            to_z[s].wait_recv()
            total = total + z_buf[batch, s].astype(f32)
        sum_buf[batch] = total.astype(bf16)

    to_weights.wait()
    for k in range(CHUNKS):
        to_near[k].wait_recv()
    down(0, near, y)
    near_x = start_x(0)
    near_z = start_z(0, near_x)
    passed = []
    for k in range(CHUNKS):
        to_far_act[k].wait_recv()
        block = far_act.at[core, chunk(k)]
        passed.append(send(block, block, pass_sems, k, column[0]))
    for copy in pages:
        copy.wait_recv()
    row_pages = [
        send(
            arrived.at[pl.ds(column[s]["row"] * group, group)],
            moved_ref.at[row], row_page_sems, s, column[s],
        )
        for s in range(rows - 1)
    ]
    for copy in passed:
        copy.wait_recv()
    down(1, far_act, 1 - y)
    far_x = start_x(1)
    finish(0, near_x, near_z)
    to_row = [send(sum_buf.at[0, 1 - core], out_ref.at[row], row_sems, 0, column[0])]
    out_ref[row] = sum_buf[0, core]
    far_z = start_z(1, far_x)
    for i in range(group):
        moved_ref[row, i] = arrived[row * group + i]
    finish(1, far_x, far_z)
    to_row.append(send(sum_buf.at[1, core], out_ref.at[row], row_sems, 1, column[1]))
    to_row.append(send(sum_buf.at[1, 1 - core], out_ref.at[row], row_sems, 2, column[2]))
    for copy in to_row + row_pages:
        copy.wait_recv()
    for copy in sent:
        copy.wait_send()


def run_experts(rows, cols, plans, part, pages, w_down, collective_id):
    groups, _, pairs, width = part.shape
    tokens = pairs // TOP
    depth = w_down.shape[2]
    share = tokens // cols
    half = cols // 2
    w_down = w_down.transpose(0, 2, 1)
    dma = pltpu.SemaphoreType.DMA
    vmem = pl.BlockSpec(memory_space=pltpu.VMEM)
    block = (groups // 2, share, depth)
    return pl.pallas_call(
        functools.partial(experts_body, rows, cols),
        out_shape=(
            jax.ShapeDtypeStruct((rows, share, depth), bf16),
            jax.ShapeDtypeStruct((rows, cols // rows) + pages.shape[1:], bf16),
        ),
        in_specs=[
            vmem, vmem, vmem, pl.BlockSpec(memory_space=pl.ANY),
        ],
        out_specs=(vmem, vmem),
        scratch_shapes=[
            pltpu.VMEM(w_down.shape, bf16),
            pltpu.VMEM((2, pairs, width), bf16),
            pltpu.VMEM((2, pairs, width), bf16),
            pltpu.VMEM((2, 2, pairs, width), bf16),
            pltpu.VMEM((2, pairs, width), bf16),
            pltpu.VMEM((2, pairs, width), bf16),
            pltpu.VMEM(pages.shape, bf16),
            pltpu.VMEM((2 * CAP, width), bf16),
            pltpu.VMEM((2, E * CAP, depth), bf16),
            pltpu.VMEM((2, E * CAP, tokens), bf16),
            pltpu.VMEM((2, groups // 2, cols, share, depth), bf16),
            pltpu.VMEM((2, half) + block, bf16),
            pltpu.VMEM((2, half - 1) + block, bf16),
            pltpu.VMEM((2, half - 1) + block, bf16),
            pltpu.VMEM((2,) + block, bf16),
            dma((2, 2 * CHUNKS)), dma((2, CHUNKS)), dma((2, CHUNKS)), dma((2, CHUNKS)),
            dma((2, CHUNKS)), dma((2, cols)), dma((2, rows)),
            dma((2, 2 * half)), dma((2, 2 * half)), dma((2, rows)), dma,
        ],
        compiler_params=pltpu.CompilerParams(
            collective_id=collective_id, has_side_effects=True, vmem_limit_bytes=38 << 20
        ),
    )(plans, part, pages, w_down)


def shards(
    row_count,
    col_count,
    residual_in,
    queries,
    fresh_cache,
    cache_pool,
    page_table,
    context,
    out_weight,
    norm_gain,
    w_gate,
    w_up,
    w_down,
    routes,
    route_weight,
    finished_pool,
    finished_table,
    finished_dest,
):
    share, width = residual_in.shape
    depth = width // row_count
    partial_value, picked, plan = attend(
        queries, fresh_cache, cache_pool, page_table, context, out_weight, routes, route_weight,
        finished_pool, finished_table, finished_dest,
    )
    hidden, tokens, plans = make_hidden(
        row_count,
        col_count,
        partial_value.reshape(col_count, share, width),
        residual_in,
        norm_gain.reshape(1, width),
        plan,
        0,
    )
    starts = plans[:, 2 * E : 3 * E, 0].astype(jnp.int32).reshape(-1)
    tokens = tokens.reshape(row_count, col_count * share, depth)
    part = gate_up(starts, plans, tokens, w_gate, w_up)
    pages = picked.reshape((col_count, picked.shape[0] // col_count) + picked.shape[1:])
    blocks, moved = run_experts(
        row_count, col_count, plans, part, pages, w_down, 1
    )
    _, group, requests, sides, block_count, heads, extent = moved.shape
    migrated = moved.transpose(3, 2, 0, 4, 1, 5, 6)
    migrated = migrated.reshape(sides, requests, row_count * block_count, group * heads, extent)
    mixture = blocks.transpose(1, 0, 2).reshape(share, width).astype(f32)
    layer_out = (hidden.astype(f32) + mixture).astype(bf16)
    return (layer_out, migrated)


def solution(mesh):
    return jax.shard_map(
        functools.partial(shards, mesh.shape["row"], mesh.shape["col"]),
        mesh=mesh,
        in_specs=(
            P(("row", "col"), None),
            P("row", "col"),
            P(None, "row", "col"),
            P(None, "row", "col", None),
            P("row", None),
            P("row"),
            P("col", None),
            P(),
            P(None, "row", "col"),
            P(None, "row", "col"),
            P(None, "col", "row"),
            P("row", None),
            P("row", None),
            P(None, "row", "col", None),
            P(None, "row"),
            P(),
        ),
        out_specs=(P(("row", "col"), None), P(None, "col", None, "row", None)),
        check_vma=False,
    )
```

```python
import functools
import math

import jax
import jax.numpy as jnp
from jax import lax
from jax.experimental import pallas as pl
from jax.experimental.pallas import tpu as pltpu
from jax.sharding import PartitionSpec as P

HD = 64
E = 8
TOP = 2
PAGE = 128
MAXP = 32
SPAN = 256
CAP = 128
WIN = CAP + 16

masked_score = -1e30
norm_eps = 1e-05
MESH = pl.DeviceIdType.MESH
f32 = jnp.float32
bf16 = jnp.bfloat16


QB = 256
STEP = 8
PAIRS = PAGE // 2

def make_plan(routes, weights):
    tokens = routes.shape[1]
    experts = lax.broadcasted_iota(jnp.int32, (E, tokens), 0)
    named = [routes[k : k + 1, :] == experts for k in range(TOP)]
    is_member = functools.reduce(jnp.logical_or, named)
    member = is_member.astype(f32).astype(bf16)
    by_expert = sum(jnp.where(named[k], weights[k : k + 1, :], 0.0) for k in range(TOP))
    before = (
        lax.broadcasted_iota(jnp.int32, (tokens, tokens), 0)
        < lax.broadcasted_iota(jnp.int32, (tokens, tokens), 1)
    ).astype(f32).astype(bf16)
    rank = jnp.dot(member, before, preferred_element_type=f32)
    lower = (
        lax.broadcasted_iota(jnp.int32, (E, E), 0) > lax.broadcasted_iota(jnp.int32, (E, E), 1)
    ).astype(f32).astype(bf16)
    ahead = jnp.dot(lower, member, preferred_element_type=f32)
    offsets = jnp.sum(ahead, axis=1, keepdims=True)
    starts = jnp.minimum(jnp.floor(offsets * (1.0 / 16)) * 16.0, tokens * TOP - WIN)
    ranks = jnp.where(is_member, rank + (offsets - starts), -1.0)
    return jnp.concatenate(
        [
            ranks,
            by_expert,
            jnp.broadcast_to(starts, ranks.shape),
            jnp.broadcast_to(offsets, ranks.shape),
        ],
        axis=0,
    )


def attend_body(
    ctx_ref, table_ref, ftable_ref, fdest_ref, q_ref, fresh_ref, weight_ref, routes_ref,
    route_weight_ref, cache_ref, pool_ref, part_ref, pages_ref, plan_ref,
    raw, picked, flat, heads_buf, out_buf, raw_sems, page_sem,
):
    head_count = cache_ref.shape[2]
    per = 8 // head_count
    blocks, finished = ftable_ref.shape

    def fetch(j, carry):
        page = table_ref[0, j]
        for kv in range(2):
            pltpu.make_async_copy(
                cache_ref.at[kv, page], raw.at[kv, j], raw_sems.at[kv, lax.div(j, STEP)]
            ).start()
        return carry

    lax.fori_loop(0, MAXP, fetch, 0, unroll=STEP)

    def regroup(f, carry):
        dest = fdest_ref[f]
        for kv in range(2):
            for b in range(blocks):
                pltpu.make_async_copy(
                    pool_ref.at[kv, ftable_ref[b, f]], picked.at[dest, kv, b], page_sem
                ).start()
        return carry

    lax.fori_loop(0, finished, regroup, 0)

    plan_ref[...] = make_plan(routes_ref[...], route_weight_ref[...])

    def spread(kv, first):
        for i in range(per):
            page = raw[kv, first + i].astype(f32)
            for t in range(PAIRS):
                flat[pl.ds(8 * t + i * head_count, head_count), :] = page[:, t * 128 : (t + 1) * 128]
        for i in range(per):
            for h in range(head_count):
                rows = flat[pl.ds(i * head_count + h, PAIRS, stride=8), :]
                where = pl.ds(pl.multiple_of((first + i) * PAIRS, PAIRS), PAIRS)
                heads_buf[kv, h, where, :] = rows.astype(bf16)

    for chunk in range(MAXP // STEP):
        for kv in range(2):
            pltpu.make_async_copy(
                raw.at[kv, pl.ds(chunk * STEP, STEP)],
                raw.at[kv, pl.ds(chunk * STEP, STEP)],
                raw_sems.at[kv, chunk],
            ).wait()

            @pl.loop(0, STEP // per)
            def _(g):
                spread(kv, chunk * STEP + g * per)

    pltpu.make_async_copy(picked, picked, page_sem).wait()
    to_pages = pltpu.make_async_copy(picked, pages_ref, page_sem)
    to_pages.start()
    context = ctx_ref[0]
    cached = MAXP * PAIRS
    scale = 1.0 / math.sqrt(HD)
    lanes = lax.broadcasted_iota(jnp.int32, (QB, 128), 1)
    low = lanes < HD
    column = lax.broadcasted_iota(jnp.int32, (QB, cached), 1)
    keep = [2 * column + p < context for p in range(2)]
    for block in range(SPAN // QB):
        rows = pl.ds(block * QB, QB)
        causal = (
            block * QB + lax.broadcasted_iota(jnp.int32, (QB, SPAN), 0)
            >= lax.broadcasted_iota(jnp.int32, (QB, SPAN), 1)
        )

        for pair in range((head_count + 1) // 2):
            lane = pl.ds(pair * 128, 128)
            both = q_ref[rows, lane].astype(f32) * scale
            turned = pltpu.roll(both, HD, 1)
            made = []
            for side in range(min(2, head_count - 2 * pair)):
                h = pair * 2 + side
                own = low if side == 0 else jnp.logical_not(low)
                straight = jnp.where(own, both, 0.0).astype(bf16)
                swapped = jnp.where(own, 0.0, turned).astype(bf16)
                by_parity = (straight, swapped) if side == 0 else (swapped, straight)
                keys = heads_buf[0, h]
                values = heads_buf[1, h]
                dims = (((1,), (1,)), ((), ()))
                s = [
                    jnp.where(
                        keep[p],
                        lax.dot_general(by_parity[p], keys, dims, preferred_element_type=f32),
                        masked_score,
                    )
                    for p in range(2)
                ]
                s_new = jnp.where(
                    causal,
                    lax.dot_general(straight, fresh_ref[0, :, lane], dims, preferred_element_type=f32),
                    masked_score,
                )
                highest = jnp.maximum(
                    jnp.max(jnp.maximum(s[0], s[1]), axis=1, keepdims=True),
                    jnp.max(s_new, axis=1, keepdims=True),
                )
                e = [jnp.exp(v - highest) for v in s]
                e_new = jnp.exp(s_new - highest)
                total = jnp.sum(e[0] + e[1], axis=1, keepdims=True) + jnp.sum(
                    e_new, axis=1, keepdims=True
                )
                o = [
                    jnp.dot(e[p].astype(bf16), values, preferred_element_type=f32)
                    for p in range(2)
                ]
                o_new = jnp.dot(
                    e_new.astype(bf16), fresh_ref[1, :, lane], preferred_element_type=f32
                )
                if side == 0:
                    o_cached = o[0] + pltpu.roll(o[1], HD, 1)
                else:
                    o_cached = o[1] + pltpu.roll(o[0], HD, 1)
                made.append((o_cached + o_new) / total)
            out_buf[rows, lane] = jnp.where(low, made[0], made[-1]).astype(bf16)
    part_ref[...] = jnp.dot(out_buf[...], weight_ref[...], preferred_element_type=f32).astype(bf16)
    to_pages.wait()


def attend(
    queries, fresh_cache, cache_pool, page_table, context, out_weight, routes, route_weight,
    finished_pool, finished_table, finished_dest,
):
    head_count = cache_pool.shape[2]
    extent = cache_pool.shape[3]
    finished, blocks = finished_table.shape
    odd = (head_count % 2) * HD
    queries = jnp.pad(queries, ((0, 0), (0, odd)))
    fresh_cache = jnp.pad(fresh_cache, ((0, 0), (0, 0), (0, odd)))
    out_weight = jnp.pad(out_weight, ((0, odd), (0, 0)))
    width = out_weight.shape[1]
    dma = pltpu.SemaphoreType.DMA
    vmem = pl.BlockSpec(memory_space=pltpu.VMEM)
    smem = pl.BlockSpec(memory_space=pltpu.SMEM)
    hbm = pl.BlockSpec(memory_space=pl.ANY)
    return pl.pallas_call(
        attend_body,
        out_shape=(
            jax.ShapeDtypeStruct((SPAN, width), bf16),
            jax.ShapeDtypeStruct((finished, 2, blocks, head_count, extent), bf16),
            jax.ShapeDtypeStruct((4 * E, SPAN), f32),
        ),
        in_specs=[smem] * 4 + [vmem] * 5 + [hbm] * 2,
        out_specs=(vmem, hbm, vmem),
        scratch_shapes=[
            pltpu.VMEM((2, MAXP, head_count, extent), bf16),
            pltpu.VMEM((finished, 2, blocks, head_count, extent), bf16),
            pltpu.VMEM((8 * PAIRS, 128), f32),
            pltpu.VMEM((2, head_count, MAXP * PAIRS, 128), bf16),
            pltpu.VMEM(queries.shape, bf16),
            dma((2, MAXP // STEP)), dma,
        ],
        compiler_params=pltpu.CompilerParams(vmem_limit_bytes=60 << 20),
    )(context, page_table, finished_table.T, finished_dest, queries, fresh_cache, out_weight,
      routes.T, route_weight.T, cache_pool, finished_pool)


def remote(src, dst, sems, index, where):
    copy = pltpu.make_async_remote_copy(
        src_ref=src,
        dst_ref=dst,
        send_sem=sems.at[0, index],
        recv_sem=sems.at[1, index],
        device_id=where,
        device_id_type=MESH,
    )
    copy.start()
    return copy


def turns(half):
    return list(range(half // 2, half)) + list(range(1, half // 2)) + [0]


def turned(place, turn, half):
    total, bit = 0, 1
    while bit < half:
        digit = place // bit % 2
        total = total + bit * (1 - digit if turn // bit % 2 else digit)
        bit *= 2
    return total


def greet(rows, cols):
    row, col = lax.axis_index("row"), lax.axis_index("col")
    a, b = col // 2, col % 2
    mate = {"col": a * 2 + (1 - b)}
    line = [{"col": turned(a, t, cols // 2) * 2 + b} for t in turns(cols // 2)[:-1]]
    column = [{"row": lax.rem(row + 1 + s, rows)} for s in range(rows - 1)]
    barrier = pltpu.get_barrier_semaphore()
    peers = [mate] + line + column
    for peer in peers:
        pl.semaphore_signal(barrier, inc=1, device_id=peer, device_id_type=MESH)
    pl.semaphore_wait(barrier, len(peers))
    return row, col, mate, line, column


def start_mates(cols, block, mate_buf, mate_sems, mate):
    col = lax.axis_index("col")
    a, b = col // 2, col % 2
    return [
        remote(
            block(turned(a, t, cols // 2) * 2 + (1 - b)), mate_buf.at[s], mate_sems, s, mate
        )
        for s, t in enumerate(turns(cols // 2))
    ]


def sum_cols(cols, load, to_mate, mate_buf, pair_buf, far_buf, far_sems, line):
    col = lax.axis_index("col")
    a, b = col // 2, col % 2
    half = cols // 2
    to_far = []
    for s in range(half - 1):
        to_mate[s].wait_recv()
        mine = load(turned(a, turns(half)[s], half) * 2 + b)
        pair_buf[s] = (mine.astype(f32) + mate_buf[s].astype(f32)).astype(bf16)
        to_far.append(remote(pair_buf.at[s], far_buf.at[s], far_sems, s, line[s]))
    to_mate[half - 1].wait_recv()
    total = load(col).astype(f32) + mate_buf[half - 1].astype(f32)
    for s in range(half - 1):
        to_far[s].wait_recv()
        total = total + far_buf[s].astype(f32)
    return total, to_far


PIECES = 2


def hidden_body(
    rows, cols, part_ref, res_ref, gain_ref, plan_ref, hidden_ref, tokens_ref, plans_ref,
    mate_buf, pair_buf, far_buf, norm_buf,
    mate_sems, far_sems, row_sems, line_sems, pass_sems, plan_sems,
):
    half = cols // 2
    depth = tokens_ref.shape[3]
    row, col, mate, line, column = greet(rows, cols)
    a, b = col // 2, col % 2
    copies = start_mates(cols, lambda i: part_ref.at[i], mate_buf, mate_sems, mate)
    to_mate = list(copies)
    plans = [
        remote(plan_ref, plans_ref.at[row], plan_sems, s, column[s]) for s in range(rows - 1)
    ]
    plans_ref[row] = plan_ref[...]
    total, to_far = sum_cols(
        cols, lambda i: part_ref[i], to_mate, mate_buf, pair_buf, far_buf, far_sems, line
    )
    hidden = (res_ref[...].astype(f32) + total).astype(bf16)
    hidden_ref[...] = hidden
    values = hidden.astype(f32)
    meansq = jnp.mean(values * values, axis=-1, keepdims=True)
    normed = (values * lax.rsqrt(meansq + norm_eps) * gain_ref[...].astype(f32)).astype(bf16)
    for r in range(rows):
        norm_buf[r] = normed[:, r * depth : (r + 1) * depth]
    to_row = [
        remote(norm_buf.at[column[s]["row"]], tokens_ref.at[row, col], row_sems, s, column[s])
        for s in range(rows - 1)
    ]
    tokens_ref[row, col] = norm_buf[row]
    for copy in to_row:
        copy.wait_recv()
    line = [{"col": lax.rem(a + 1 + s, half) * 2 + b} for s in range(half - 1)]
    cut = rows // PIECES

    def piece(p, origin):
        return tokens_ref.at[pl.ds(p * cut, cut), origin]

    to_line = [
        remote(piece(p, col), piece(p, col), line_sems, p * half + s, line[s])
        for p in range(PIECES)
        for s in range(half - 1)
    ]
    passed = [
        remote(piece(p, col), piece(p, col), pass_sems, p * half + half - 1, mate)
        for p in range(PIECES)
    ]
    for p in range(PIECES):
        for s in range(half - 1):
            to_line[p * (half - 1) + s].wait_recv()
            origin = lax.rem(a - 1 - s + half, half) * 2 + b
            passed.append(
                remote(piece(p, origin), piece(p, origin), pass_sems, p * half + s, mate)
            )
    for copy in passed:
        copy.wait_recv()
    for copy in plans:
        copy.wait_recv()
    for copy in to_mate + plans + to_far + to_row + to_line + passed:
        copy.wait_send()


def make_hidden(rows, cols, part, residual, gain, plan, collective_id):
    share, width = residual.shape
    depth = width // rows
    half = cols // 2
    dma = pltpu.SemaphoreType.DMA
    vmem = pl.BlockSpec(memory_space=pltpu.VMEM)
    return pl.pallas_call(
        functools.partial(hidden_body, rows, cols),
        out_shape=(
            jax.ShapeDtypeStruct((share, width), bf16),
            jax.ShapeDtypeStruct((rows, cols, share, depth), bf16),
            jax.ShapeDtypeStruct((rows,) + plan.shape, f32),
        ),
        in_specs=[vmem] * 4,
        out_specs=(vmem, vmem, vmem),
        scratch_shapes=[
            pltpu.VMEM((half, share, width), bf16),
            pltpu.VMEM((half - 1, share, width), bf16),
            pltpu.VMEM((half - 1, share, width), bf16),
            pltpu.VMEM((rows, share, depth), bf16),
            dma((2, half)), dma((2, half)), dma((2, rows)), dma((2, PIECES * half)),
            dma((2, PIECES * half)),
            dma((2, rows)),
        ],
        compiler_params=pltpu.CompilerParams(
            collective_id=collective_id, has_side_effects=True, vmem_limit_bytes=32 << 20
        ),
    )(part, residual, gain, plan)


def gate_up_body(start_ref, plan_ref, x_ref, gate_ref, up_ref, out_ref, rows_ref):
    e = pl.program_id(0)
    groups, tokens = x_ref.shape[0], x_ref.shape[1]

    @pl.when(e == 0)
    def _():
        out_ref[...] = jnp.zeros_like(out_ref)

    slots = lax.broadcasted_iota(jnp.int32, (WIN, tokens), 0).astype(f32)
    for r in range(groups):
        pick = (slots == plan_ref[r, pl.ds(e, 1), :]).astype(f32).astype(bf16)
        rows_ref[r * WIN : (r + 1) * WIN, :] = jnp.dot(
            pick, x_ref[r], preferred_element_type=f32
        ).astype(bf16)
    for side, weight in enumerate((gate_ref, up_ref)):
        sums = jnp.dot(rows_ref[...], weight[0], preferred_element_type=f32).astype(bf16)
        for r in range(groups):
            window = pl.ds(pl.multiple_of(start_ref[r * E + e], 16), WIN)
            out_ref[r, side, window, :] += sums[r * WIN : (r + 1) * WIN]


def gate_up(starts, plans, x, w_gate, w_up):
    groups, tokens, depth = x.shape
    width = w_gate.shape[2]
    weight_spec = pl.BlockSpec((1, depth, width), lambda e, s: (e, 0, 0))
    return pl.pallas_call(
        gate_up_body,
        grid_spec=pltpu.PrefetchScalarGridSpec(
            num_scalar_prefetch=1,
            grid=(E,),
            in_specs=[
                pl.BlockSpec(plans.shape, lambda e, s: (0, 0, 0)),
                pl.BlockSpec((groups, tokens, depth), lambda e, s: (0, 0, 0)),
                weight_spec,
                weight_spec,
            ],
            out_specs=pl.BlockSpec((groups, 2, tokens * TOP, width), lambda e, s: (0, 0, 0, 0)),
            scratch_shapes=[pltpu.VMEM((groups * WIN, depth), bf16)],
        ),
        out_shape=jax.ShapeDtypeStruct((groups, 2, tokens * TOP, width), bf16),
        compiler_params=pltpu.CompilerParams(vmem_limit_bytes=44 << 20),
    )(starts, plans, x, w_gate, w_up)


CHUNKS = 4


def experts_body(
    rows, cols, plan_ref, part_ref, pages_ref, down_ref,
    out_ref, moved_ref,
    weights, near, far_act, mate_buf, far_out, far_buf, arrived, rows_buf, outs_buf, mix_buf,
    mixed, x_buf, pair_buf, z_buf, sum_buf,
    mate_sems, far_sems, near_sems, far_act_sems, pass_sems, col_sems, row_page_sems,
    x_sems, z_sems, row_sems, weight_sem,
):
    row, col = lax.axis_index("row"), lax.axis_index("col")
    y, core = row // 2, row % 2
    mate, far, diag = y * 2 + (1 - core), (1 - y) * 2 + core, (1 - y) * 2 + (1 - core)
    half = cols // 2
    group = cols // rows
    a, b = col // 2, col % 2
    x_mate = {"col": a * 2 + (1 - b)}
    line = [{"col": turned(a, t, half) * 2 + b} for t in turns(half)[:-1]]
    column = [{"row": r} for r in (mate, far, diag)]
    others = [lax.rem(col + 1 + s, cols) for s in range(cols - 1)]
    height = part_ref.shape[2] // CHUNKS
    share, depth = out_ref.shape[1], out_ref.shape[2]

    to_weights = pltpu.make_async_copy(down_ref, weights, weight_sem)
    to_weights.start()
    barrier = pltpu.get_barrier_semaphore()
    peers = column + [{"col": c} for c in others]
    for peer in peers:
        pl.semaphore_signal(barrier, inc=1, device_id=peer, device_id_type=MESH)
    pl.semaphore_wait(barrier, len(peers))
    sent = []

    def send(src, dst, sems, index, where):
        copy = remote(src, dst, sems, index, where)
        sent.append(copy)
        return copy

    def chunk(k):
        return pl.ds(k * height, height)

    def start_mate(which, side, k):
        return send(
            part_ref.at[side * 2 + (1 - core), :, chunk(k)],
            mate_buf.at[which, :, chunk(k)],
            mate_sems, which * CHUNKS + k, column[0],
        )

    to_mate = [[start_mate(0, 1 - y, k) for k in range(CHUNKS)], []]
    to_far = []
    for k in range(CHUNKS):
        to_mate[0][k].wait_recv()
        far_out[:, chunk(k), :] = (
            part_ref[far, :, chunk(k), :].astype(f32) + mate_buf[0, :, chunk(k), :].astype(f32)
        ).astype(bf16)
        to_far.append(
            send(far_out.at[:, chunk(k)], far_buf.at[:, chunk(k)], far_sems, k, column[1])
        )
        to_mate[1].append(start_mate(1, y, k))
    pages = [
        send(pages_ref.at[c], arrived.at[col], col_sems, s, {"col": c})
        for s, c in enumerate(others)
    ]
    arrived[col] = pages_ref[col]
    to_near, to_far_act = [], []
    for k in range(CHUNKS):
        to_mate[1][k].wait_recv()
        to_far[k].wait_recv()
        sums = [
            part_ref[row, s, chunk(k), :].astype(f32)
            + mate_buf[1, s, chunk(k), :].astype(f32)
            + far_buf[s, chunk(k), :].astype(f32)
            for s in range(2)
        ]
        near[core, chunk(k), :] = (sums[0] / (1.0 + jnp.exp(-sums[0])) * sums[1]).astype(bf16)
        block = near.at[core, chunk(k)]
        to_far_act.append(send(block, far_act.at[core, chunk(k)], far_act_sems, k, column[1]))
        to_near.append(send(block, near.at[core, chunk(k)], near_sems, k, column[0]))

    pairs, tokens = near.shape[1], mix_buf.shape[2]
    slots = lax.broadcasted_iota(jnp.int32, (CAP, tokens), 0).astype(f32)
    ahead = (
        lax.broadcasted_iota(jnp.int32, (CAP, pairs), 1)
        - lax.broadcasted_iota(jnp.int32, (CAP, pairs), 0)
    ).astype(f32)

    def down(batch, act, side):
        @pl.loop(0, E)
        def _(e):
            for c in range(2):
                offset = plan_ref[side * 2 + c, pl.ds(3 * E + e, 1), :]
                offset = jnp.concatenate([offset] * TOP, axis=1)
                pick = (ahead == offset).astype(f32).astype(bf16)
                rows_buf[c * CAP : (c + 1) * CAP, :] = jnp.dot(
                    pick, act[c], preferred_element_type=f32
                ).astype(bf16)
            outs = lax.dot_general(
                rows_buf[...], weights[e], (((1,), (1,)), ((), ())), preferred_element_type=f32
            ).astype(bf16)
            place = pl.ds(pl.multiple_of(e * CAP, CAP), CAP)
            for c in range(2):
                r = side * 2 + c
                outs_buf[c, place, :] = outs[c * CAP : (c + 1) * CAP]
                shift = (
                    plan_ref[r, pl.ds(3 * E + e, 1), :] - plan_ref[r, pl.ds(2 * E + e, 1), :]
                )
                mix_buf[c, place, :] = jnp.where(
                    slots == plan_ref[r, pl.ds(e, 1), :] - shift,
                    plan_ref[r, pl.ds(E + e, 1), :],
                    0.0,
                ).astype(bf16)

        for c in range(2):
            total = lax.dot_general(
                mix_buf[c], outs_buf[c], (((0,), (0,)), ((), ())), preferred_element_type=f32
            ).astype(bf16)
            mixed[batch, c] = total.reshape(cols, share, depth)

    def start_x(batch):
        return [
            send(
                mixed.at[batch, :, turned(a, t, half) * 2 + (1 - b)],
                x_buf.at[batch, s], x_sems, batch * half + s, x_mate,
            )
            for s, t in enumerate(turns(half))
        ]

    def start_z(batch, to_x):
        to_z = []
        for s in range(half - 1):
            to_x[s].wait_recv()
            mine = mixed[batch, :, turned(a, turns(half)[s], half) * 2 + b]
            pair_buf[batch, s] = (mine.astype(f32) + x_buf[batch, s].astype(f32)).astype(bf16)
            to_z.append(
                send(
                    pair_buf.at[batch, s], z_buf.at[batch, s],
                    z_sems, batch * half + s, line[s],
                )
            )
        return to_z

    def finish(batch, to_x, to_z):
        to_x[half - 1].wait_recv()
        total = mixed[batch, :, col].astype(f32) + x_buf[batch, half - 1].astype(f32)
        for s in range(half - 1):
            to_z[s].wait_recv()
            total = total + z_buf[batch, s].astype(f32)
        sum_buf[batch] = total.astype(bf16)

    to_weights.wait()
    for k in range(CHUNKS):
        to_near[k].wait_recv()
    down(0, near, y)
    near_x = start_x(0)
    near_z = start_z(0, near_x)
    passed = []
    for k in range(CHUNKS):
        to_far_act[k].wait_recv()
        block = far_act.at[core, chunk(k)]
        passed.append(send(block, block, pass_sems, k, column[0]))
    for copy in pages:
        copy.wait_recv()
    row_pages = [
        send(
            arrived.at[pl.ds(column[s]["row"] * group, group)],
            moved_ref.at[row], row_page_sems, s, column[s],
        )
        for s in range(rows - 1)
    ]
    for copy in passed:
        copy.wait_recv()
    down(1, far_act, 1 - y)
    far_x = start_x(1)
    finish(0, near_x, near_z)
    to_row = [send(sum_buf.at[0, 1 - core], out_ref.at[row], row_sems, 0, column[0])]
    out_ref[row] = sum_buf[0, core]
    far_z = start_z(1, far_x)
    for i in range(group):
        moved_ref[row, i] = arrived[row * group + i]
    finish(1, far_x, far_z)
    to_row.append(send(sum_buf.at[1, core], out_ref.at[row], row_sems, 1, column[1]))
    to_row.append(send(sum_buf.at[1, 1 - core], out_ref.at[row], row_sems, 2, column[2]))
    for copy in to_row + row_pages:
        copy.wait_recv()
    for copy in sent:
        copy.wait_send()


def run_experts(rows, cols, plans, part, pages, w_down, collective_id):
    groups, _, pairs, width = part.shape
    tokens = pairs // TOP
    depth = w_down.shape[2]
    share = tokens // cols
    half = cols // 2
    w_down = w_down.transpose(0, 2, 1)
    dma = pltpu.SemaphoreType.DMA
    vmem = pl.BlockSpec(memory_space=pltpu.VMEM)
    block = (groups // 2, share, depth)
    return pl.pallas_call(
        functools.partial(experts_body, rows, cols),
        out_shape=(
            jax.ShapeDtypeStruct((rows, share, depth), bf16),
            jax.ShapeDtypeStruct((rows, cols // rows) + pages.shape[1:], bf16),
        ),
        in_specs=[
            vmem, vmem, vmem, pl.BlockSpec(memory_space=pl.ANY),
        ],
        out_specs=(vmem, vmem),
        scratch_shapes=[
            pltpu.VMEM(w_down.shape, bf16),
            pltpu.VMEM((2, pairs, width), bf16),
            pltpu.VMEM((2, pairs, width), bf16),
            pltpu.VMEM((2, 2, pairs, width), bf16),
            pltpu.VMEM((2, pairs, width), bf16),
            pltpu.VMEM((2, pairs, width), bf16),
            pltpu.VMEM(pages.shape, bf16),
            pltpu.VMEM((2 * CAP, width), bf16),
            pltpu.VMEM((2, E * CAP, depth), bf16),
            pltpu.VMEM((2, E * CAP, tokens), bf16),
            pltpu.VMEM((2, groups // 2, cols, share, depth), bf16),
            pltpu.VMEM((2, half) + block, bf16),
            pltpu.VMEM((2, half - 1) + block, bf16),
            pltpu.VMEM((2, half - 1) + block, bf16),
            pltpu.VMEM((2,) + block, bf16),
            dma((2, 2 * CHUNKS)), dma((2, CHUNKS)), dma((2, CHUNKS)), dma((2, CHUNKS)),
            dma((2, CHUNKS)), dma((2, cols)), dma((2, rows)),
            dma((2, 2 * half)), dma((2, 2 * half)), dma((2, rows)), dma,
        ],
        compiler_params=pltpu.CompilerParams(
            collective_id=collective_id, has_side_effects=True, vmem_limit_bytes=38 << 20
        ),
    )(plans, part, pages, w_down)


def lay_out_body(moved_ref, out_ref):
    _, group, requests, _, blocks, heads, _ = moved_ref.shape
    for q in range(requests):
        for k in range(blocks):
            parts = [moved_ref[0, c, q, 0, k].astype(f32) for c in range(group)]
            out_ref[0, q, k] = jnp.concatenate(parts, axis=0).astype(bf16)


def lay_out(moved):
    rows, group, requests, sides, blocks, heads, extent = moved.shape
    return pl.pallas_call(
        lay_out_body,
        grid=(sides, rows),
        out_shape=jax.ShapeDtypeStruct(
            (sides, requests, rows * blocks, group * heads, extent), bf16
        ),
        in_specs=[
            pl.BlockSpec(
                (1, group, requests, 1, blocks, heads, extent),
                lambda side, r: (r, 0, 0, side, 0, 0, 0),
            )
        ],
        out_specs=pl.BlockSpec(
            (1, requests, blocks, group * heads, extent), lambda side, r: (side, 0, r, 0, 0)
        ),
        compiler_params=pltpu.CompilerParams(vmem_limit_bytes=16 << 20),
    )(moved)


def shards(
    row_count,
    col_count,
    residual_in,
    queries,
    fresh_cache,
    cache_pool,
    page_table,
    context,
    out_weight,
    norm_gain,
    w_gate,
    w_up,
    w_down,
    routes,
    route_weight,
    finished_pool,
    finished_table,
    finished_dest,
):
    share, width = residual_in.shape
    depth = width // row_count
    partial_value, picked, plan = attend(
        queries, fresh_cache, cache_pool, page_table, context, out_weight, routes, route_weight,
        finished_pool, finished_table, finished_dest,
    )
    hidden, tokens, plans = make_hidden(
        row_count,
        col_count,
        partial_value.reshape(col_count, share, width),
        residual_in,
        norm_gain.reshape(1, width),
        plan,
        0,
    )
    starts = plans[:, 2 * E : 3 * E, 0].astype(jnp.int32).reshape(-1)
    tokens = tokens.reshape(row_count, col_count * share, depth)
    part = gate_up(starts, plans, tokens, w_gate, w_up)
    pages = picked.reshape((col_count, picked.shape[0] // col_count) + picked.shape[1:])
    blocks, moved = run_experts(
        row_count, col_count, plans, part, pages, w_down, 1
    )
    migrated = lay_out(moved)
    mixture = blocks.transpose(1, 0, 2).reshape(share, width).astype(f32)
    layer_out = (hidden.astype(f32) + mixture).astype(bf16)
    return (layer_out, migrated)


def solution(mesh):
    return jax.shard_map(
        functools.partial(shards, mesh.shape["row"], mesh.shape["col"]),
        mesh=mesh,
        in_specs=(
            P(("row", "col"), None),
            P("row", "col"),
            P(None, "row", "col"),
            P(None, "row", "col", None),
            P("row", None),
            P("row"),
            P("col", None),
            P(),
            P(None, "row", "col"),
            P(None, "row", "col"),
            P(None, "col", "row"),
            P("row", None),
            P("row", None),
            P(None, "row", "col", None),
            P(None, "row"),
            P(),
        ),
        out_specs=(P(("row", "col"), None), P(None, "col", None, "row", None)),
        check_vma=False,
    )
```
